32 devices in a mesh: req: 8 (over z, y), tp: 4 (over x, core).
Axes of the slice: x: 2, y: 2, z: 4, core: 2. Of those that a mesh axis runs over, the one named last changes fastest.
Arguments:
- tokens: bfloat16 [16, 1024], P('req'), may hold values from -4 to 4
- slot_of: int32 [16], replicated, may hold values from 0 to 15, each once
- key_cache: bfloat16 [16, 1536, 1024], P('req', None, 'tp'), may hold values from -1100 to 1100
- value_cache: bfloat16 [16, 1536, 1024], P('req', None, 'tp'), may hold values from -6 to 6
- cache_len: int32 [16], P('req'), may hold values from 1 to 1536, as said below
- rel_bucket: int32 [16, 1536], P('req'), may hold values from 0 to 511
- rel_table: bfloat16 [512, 1024], P('req'), may hold values from -6 to 6
- w_query: bfloat16 [1024, 1024], P(None, 'tp'), may hold values from -0.1875 to 0.1875
- w_key: bfloat16 [1024, 1024], P(None, 'tp'), may hold values from -0.1875 to 0.1875
- w_out: bfloat16 [1024, 1024], P('tp'), may hold values from -0.1875 to 0.1875
- out_gain: float32 [1024], P('tp'), may hold values from 0.1 to 1.9
- out_bias: float32 [1024], P('tp'), may hold values from -0.5 to 0.5
Outputs:
- normed: bfloat16 [16, 1024], P('req', 'tp')
The draws below stay inside these ranges and needn't reach their ends.
Inputs may be any that keep to these rules, and one draw needn't show every extreme that they name: slot_of names every slot exactly once. `cache_len`: some slot holds exactly 1536 live positions in every draw.
All inputs are finite; a program needn't handle non-finite values.
Results may differ from the reference program's by a relative error of at most 0.0034.
The reference program's roundings to bfloat16 on the way (of `rel_norm`, `rel_key`, `rel_query`, `queries`, `weights` and `context`) count: a program that leaves them out, or rounds other values in their place, can miss the bound.
Values may be sent and summed in bfloat16 or wider, within the bound.
No kernel may reach another device: no remote copies, remote signals or barrier semaphores. Data moves between devices by JAX's collectives and lax.ppermute only.
A program may use at most 64 MiB of HBM per device.

```python
import math
import jax
import jax.numpy as jnp
from jax import lax

D = 1024
HEADS = 16
HD = 64
BUCKETS = 512
MAXLEN = 1536
REQS = 16


def draw_key_cache(key, part):
    key_base = jax.random.fold_in(jax.random.fold_in(key, 11), 0)
    base = jnp.clip(jax.random.normal(key_base, (REQS, MAXLEN, D), jnp.float32), -6.0, 6.0) * 3.0
    return base.astype(jnp.bfloat16)


def draw_cache_len(key, part):
    key_first, key_second, key_full = jax.random.split(jax.random.fold_in(key, 23), 3)
    first_len = jax.random.randint(key_first, (REQS,), 1, MAXLEN + 1)
    second_len = jax.random.randint(key_second, (REQS,), 1, MAXLEN + 1)
    lengths = jnp.minimum(first_len, second_len)
    full_slot = jax.random.randint(key_full, (), 0, REQS)
    return jnp.where(jnp.arange(REQS) == full_slot, MAXLEN, lengths).astype(jnp.int32)


def with_ends(result, stream_key, smallest, largest):
    longest = result.shape.index(max(result.shape))
    spots = []
    for shift in (0, 1):
        where = [jax.random.randint(jax.random.fold_in(stream_key, axis), (), 0, length) for axis, length in enumerate(result.shape)]
        where[longest] = (where[longest] + shift) % result.shape[longest]
        spots.append(tuple(where))
    return result.at[spots[0]].set(smallest).at[spots[1]].set(largest)


def steps_of(own_key, dims, shards, low, largest):
    def one(dim, blocks):
        steps = jax.random.uniform(jax.random.fold_in(jax.random.fold_in(own_key, 6), dim), (blocks,), jnp.float32, low / len(shards), largest / len(shards))
        return jnp.repeat(jnp.exp(steps), dims[dim] // blocks).reshape((-1,) + (1,) * (len(dims) - dim - 1))

    level = one(*shards[0])
    for cut in shards[1:]:
        level = level * one(*cut)
    return level


def scatter_about(stream_key, dims, scale, bound, cuts=(), kind=jnp.bfloat16):
    loudness = steps_of(stream_key, dims, cuts, -0.22, 0.18) if cuts else 1.0
    array = jax.random.normal(stream_key, dims, jnp.float32) * scale * loudness
    return jnp.minimum(jnp.maximum(array, -bound), bound).astype(kind)


def setup_inputs(seed: int = 0) -> dict:
    key_of = jax.random.split(jax.random.key(seed), 13)
    return {
        "tokens": scatter_about(key_of[0], (REQS, D), 0.3, 4.0, ((0, 8),)),
        "slot_of": jax.random.permutation(key_of[1], REQS).astype(jnp.int32),
        "key_cache": draw_key_cache(jax.random.fold_in(key_of[12], 71), 0),
        "value_cache": scatter_about(key_of[3], (REQS, MAXLEN, D), 1.0, 6.0, ((0, 8), (2, 4))),
        "cache_len": draw_cache_len(jax.random.fold_in(key_of[12], 71), 0),
        "rel_bucket": with_ends(jax.random.randint(key_of[5], (REQS, MAXLEN), 0, BUCKETS), jax.random.fold_in(key_of[5], 1), 0, BUCKETS - 1).astype(jnp.int32),
        "rel_table": scatter_about(key_of[6], (BUCKETS, D), 1.0, 6.0, ((0, 8),)),
        "w_query": scatter_about(key_of[7], (D, D), D ** -0.5, 0.1875, ((1, 4),)),
        "w_key": scatter_about(key_of[8], (D, D), D ** -0.5, 0.1875, ((1, 4),)),
        "w_out": scatter_about(key_of[9], (D, D), D ** -0.5, 0.1875, ((0, 4),)),
        "out_gain": jnp.clip(1.0 + 0.18 * jax.random.normal(key_of[10], (D,), jnp.float32), 0.1, 1.9),
        "out_bias": jnp.clip(jax.random.uniform(key_of[11], (D,), jnp.float32, -0.5, 0.5) * steps_of(key_of[11], (D,), ((0, 4),), -0.4, 0.0), -0.5, 0.5),
    }


epsilon = 1e-06
masked_score = -1e+30

def norm_rows(matrix):
    row_mean = lax.optimization_barrier(jnp.mean(matrix, axis=-1, keepdims=True))
    centred = matrix - row_mean
    variance = lax.optimization_barrier(jnp.mean(centred * centred, axis=-1, keepdims=True))
    return centred * lax.rsqrt(variance + epsilon)

def reference(tokens, slot_of, key_cache, value_cache, cache_len, rel_bucket, rel_table, w_query, w_key, w_out, out_gain, out_bias):
    rel_norm = norm_rows(rel_table.astype(jnp.float32)).astype(jnp.bfloat16)
    rel_key = jnp.dot(rel_norm, w_key, preferred_element_type=jnp.float32).astype(jnp.bfloat16)
    rel_query = jnp.dot(rel_norm, w_query, preferred_element_type=jnp.float32).astype(jnp.bfloat16)
    queries = jnp.dot(tokens, w_query, preferred_element_type=jnp.float32).astype(jnp.bfloat16)
    score_scale = 1.0 / math.sqrt(3.0 * HD)
    positions = jnp.arange(MAXLEN, dtype=jnp.int32)

    def attend(request_item):
        query_row, slot_index = request_item
        key_rows = key_cache[slot_index].astype(jnp.float32).reshape(MAXLEN, HEADS, HD)
        value_rows = value_cache[slot_index].astype(jnp.float32).reshape(MAXLEN, HEADS, HD)
        forward = rel_bucket[slot_index].astype(jnp.int32)
        backward = jnp.minimum(BUCKETS - forward, BUCKETS - 1).astype(jnp.int32)
        rows_fwd = rel_key[forward].astype(jnp.float32).reshape(MAXLEN, HEADS, HD)
        rows_back = rel_query[backward].astype(jnp.float32).reshape(MAXLEN, HEADS, HD)
        query_heads = query_row.astype(jnp.float32).reshape(HEADS, HD)
        content = jnp.einsum('hd,jhd->hj', query_heads, key_rows)
        along_key = jnp.einsum('hd,jhd->hj', query_heads, rows_fwd)
        against = lax.optimization_barrier(jnp.sum(key_rows * rows_back, axis=2)).T
        scores = (content + along_key + against) * score_scale
        live_keys = (positions < cache_len[slot_index])[None, :]
        scores = jnp.where(live_keys, scores, masked_score)
        highest = lax.optimization_barrier(jnp.max(scores, axis=1, keepdims=True))
        exponent = jnp.where(live_keys, jnp.exp(scores - highest), 0.0)
        weights = (exponent / lax.optimization_barrier(jnp.sum(exponent, axis=1, keepdims=True))).astype(jnp.bfloat16)
        context = jnp.einsum('hj,jhd->hd', weights.astype(jnp.float32), value_rows)
        return context.reshape(HEADS * HD).astype(jnp.bfloat16)
    context = lax.map(attend, (queries, slot_of))
    attended = jnp.dot(context, w_out, preferred_element_type=jnp.float32) + tokens.astype(jnp.float32)
    return (norm_rows(attended) * out_gain + out_bias).astype(jnp.bfloat16)
```

```python
import math

import jax
import jax.numpy as jnp
from jax import lax
from jax.experimental import pallas as pl
from jax.experimental.pallas import tpu as pltpu
from jax.sharding import PartitionSpec as P

HD = 64
BUCKETS = 512
MAXLEN = 1536
BLOCK = 512
LANES = 128
QROWS = 8

epsilon = 1e-06
masked_score = -1e30

NT = (((1,), (1,)), ((), ()))
VMEM = pl.BlockSpec(memory_space=pltpu.VMEM)
SMEM = pl.BlockSpec(memory_space=pltpu.SMEM)


def dot_f32(a, b):
    return jnp.dot(a, b, preferred_element_type=jnp.float32)


def dot_nt(a, b):
    return lax.dot_general(a, b, NT, preferred_element_type=jnp.float32)


def project_kernel(tokens_ref, table_ref, w_query_ref, w_key_ref, out_ref):
    peers, _, width = out_ref.shape
    cols = width // 2
    rows = table_ref.shape[0]
    rows_dev = tokens_ref.shape[0]
    first_query = out_ref.shape[1] - QROWS
    table = table_ref[...].astype(jnp.float32)
    centred = table - jnp.mean(table, axis=1, keepdims=True)
    variance = jnp.mean(centred * centred, axis=1, keepdims=True)
    normed = (centred * lax.rsqrt(variance + epsilon)).astype(jnp.bfloat16)
    rel_key = dot_f32(normed, w_key_ref[...]).astype(jnp.bfloat16)
    rel_query = dot_f32(normed, w_query_ref[...]).astype(jnp.bfloat16)
    queries = dot_f32(tokens_ref[...], w_query_ref[...])
    queries = jnp.concatenate(
        (queries, jnp.zeros((QROWS - rows_dev, cols), jnp.float32)), axis=0
    ).astype(jnp.bfloat16)
    for peer in range(peers):
        out_ref[peer, 0:rows, 0:cols] = rel_key
        out_ref[peer, 0:rows, cols:width] = rel_query
        out_ref[peer, first_query:, 0:cols] = queries
        out_ref[peer, first_query:, cols:width] = jnp.zeros_like(queries)


def split3(value):
    high = value.astype(jnp.bfloat16)
    rest = value - high.astype(jnp.float32)
    middle = rest.astype(jnp.bfloat16)
    low = (rest - middle.astype(jnp.float32)).astype(jnp.bfloat16)
    return high, middle, low


def attend_kernel(
    slot_of_ref,
    cache_len_ref,
    table_ref,
    queries_ref,
    bucket_ref,
    key_ref,
    value_ref,
    w_out_ref,
    out_ref,
    rel_key_ref,
    rel_back_ref,
    score_ref,
    part_ref,
):
    rows_dev = key_ref.shape[0]
    cols = key_ref.shape[2]
    local_heads = cols // HD
    shards, shard_rows = table_ref.shape[0], BUCKETS // table_ref.shape[0]
    requests = slot_of_ref.shape[0]
    first_slot = lax.axis_index("req") * rows_dev

    for shard in range(shards):
        at = shard * shard_rows
        rel_key_ref[at : at + shard_rows, :] = table_ref[shard, 0:shard_rows, 0:cols]
        rel_back_ref[at : at + shard_rows, :] = table_ref[shard, 0:shard_rows, cols : 2 * cols]
    forward_id = lax.broadcasted_iota(jnp.int32, (BUCKETS, BUCKETS), 0)
    table_id = lax.broadcasted_iota(jnp.int32, (BUCKETS, BUCKETS), 1)
    swap = jnp.where(jnp.minimum(BUCKETS - forward_id, BUCKETS - 1) == table_id, 1.0, 0.0)
    rel_back = dot_f32(swap.astype(jnp.bfloat16), rel_back_ref[...]).astype(jnp.bfloat16)
    rel_key = rel_key_ref[...]

    head_of_lane = lax.broadcasted_iota(jnp.int32, (8, cols), 1) // HD
    own_lane = head_of_lane == lax.broadcasted_iota(jnp.int32, (8, cols), 0)
    head_sum = jnp.where(own_lane, 1.0, 0.0).astype(jnp.bfloat16)
    lane_id = lax.broadcasted_iota(jnp.int32, (BLOCK, LANES), 1)
    scale = 1.0 / math.sqrt(3.0 * HD)

    contexts = []
    for index in range(rows_dev):
        slot = first_slot + index
        length = cache_len_ref[index]

        def find(request, found):
            return jnp.where(slot_of_ref[request] == slot, request, found)

        request = lax.fori_loop(0, requests, find, 0, unroll=min(requests, 16))
        candidates = queries_ref[request // rows_dev, queries_ref.shape[1] - QROWS :, 0:cols]
        candidates = candidates.astype(jnp.float32)
        sublane = lax.broadcasted_iota(jnp.int32, (QROWS, cols), 0)
        query = jnp.sum(
            jnp.where(sublane == request % rows_dev, candidates, 0.0), axis=0, keepdims=True
        )
        query_heads = jnp.where(own_lane, jnp.broadcast_to(query, (8, cols)), 0.0)
        query_heads = query_heads.astype(jnp.bfloat16)
        by_bucket = jnp.concatenate(split3(dot_nt(query_heads, rel_key)), axis=0)
        left = jnp.concatenate((query_heads, head_sum, head_sum), axis=1)

        score_ref[...] = jnp.full(score_ref.shape, masked_score, jnp.float32)
        for offset in range(0, MAXLEN, BLOCK):

            @pl.when(offset < length)
            def _():
                buckets = bucket_ref[index : index + 1, offset : offset + BLOCK]
                spread = jnp.broadcast_to(buckets, (LANES, BLOCK)).T
                one_hot = jnp.concatenate(
                    [
                        jnp.where(spread == lane_id + start, 1.0, 0.0).astype(jnp.bfloat16)
                        for start in range(0, BUCKETS, LANES)
                    ],
                    axis=1,
                )
                back = dot_f32(one_hot, rel_back)
                keys = key_ref[index, offset : offset + BLOCK, :]
                products = keys.astype(jnp.float32) * back
                high = products.astype(jnp.bfloat16)
                low = (products - high.astype(jnp.float32)).astype(jnp.bfloat16)
                right = jnp.concatenate((keys, high, low), axis=1)
                along = dot_nt(by_bucket, one_hot)
                block = dot_nt(left, right) + (along[0:8] + (along[8:16] + along[16:24]))
                position = lax.broadcasted_iota(jnp.int32, (8, BLOCK), 1) + offset
                score_ref[:, offset : offset + BLOCK] = jnp.where(
                    position < length, block * scale, masked_score
                )

        scores = score_ref[...]
        live = lax.broadcasted_iota(jnp.int32, scores.shape, 1) < length
        highest = jnp.max(scores, axis=1, keepdims=True)
        exponent = jnp.where(live, jnp.exp(scores - highest), 0.0)
        weights = (exponent / jnp.sum(exponent, axis=1, keepdims=True)).astype(jnp.bfloat16)
        spread_context = dot_f32(weights, value_ref[index])
        contexts.append(
            jnp.sum(jnp.where(own_lane, spread_context, 0.0), axis=0, keepdims=True)
        )

    context = jnp.concatenate(contexts, axis=0).astype(jnp.bfloat16)
    part_ref[...] = dot_f32(context, w_out_ref[...])
    chunks = part_ref.shape[1] // LANES
    packed = jnp.concatenate(
        [
            part_ref[index : index + 1, chunk * LANES : (chunk + 1) * LANES]
            for index in range(rows_dev)
            for chunk in range(chunks)
        ],
        axis=0,
    )
    out_ref[...] = jnp.broadcast_to(packed[None], out_ref.shape)


def finish_kernel(
    slot_of_ref, parts_ref, tokens_ref, gain_ref, bias_ref, out_ref, token_rows_ref, norm_ref, row_ref
):
    rows_dev, width = tokens_ref.shape
    cols = out_ref.shape[1]
    chunks = width // LANES
    tp_size = width // cols
    own_chunks = cols // LANES
    first_row = lax.axis_index("req") * rows_dev
    first_chunk = lax.axis_index("tp") * own_chunks
    tokens = tokens_ref[...].astype(jnp.float32)
    for row in range(rows_dev):
        for chunk in range(chunks):
            token_rows_ref[row * chunks + chunk : row * chunks + chunk + 1, :] = tokens[
                row : row + 1, chunk * LANES : (chunk + 1) * LANES
            ]
    for row in range(rows_dev):
        slot = slot_of_ref[first_row + row]
        start = pl.multiple_of(lax.rem(slot, rows_dev) * chunks, chunks)
        source = (slot // rows_dev) * tp_size
        total = parts_ref[source, pl.ds(start, chunks), :]
        for other in range(1, tp_size):
            total = total + parts_ref[source + other, pl.ds(start, chunks), :]
        attended = total + token_rows_ref[row * chunks : (row + 1) * chunks, :]
        mean = jnp.sum(attended, keepdims=True) / width
        centred = attended - mean
        variance = jnp.sum(centred * centred, keepdims=True) / width
        norm_ref[...] = centred * lax.rsqrt(variance + epsilon)
        for chunk in range(own_chunks):
            row_ref[row : row + 1, chunk * LANES : (chunk + 1) * LANES] = norm_ref[
                pl.ds(first_chunk + chunk, 1), :
            ]
    out_ref[...] = (row_ref[...] * gain_ref[...] + bias_ref[...]).astype(out_ref.dtype)


def make_per_device(req_size, tp_size):
    def per_device(
        tokens,
        slot_of,
        key_cache,
        value_cache,
        cache_len,
        rel_bucket,
        rel_table,
        w_query,
        w_key,
        w_out,
        out_gain,
        out_bias,
    ):
        rows_dev, width = tokens.shape
        cols = w_query.shape[1]
        shard_rows = rel_table.shape[0]
        table_rows = -(-shard_rows // 8) * 8
        block_rows = table_rows + QROWS
        send = pl.pallas_call(
            project_kernel,
            out_shape=jax.ShapeDtypeStruct((req_size, block_rows, 2 * cols), jnp.bfloat16),
            in_specs=[VMEM] * 4,
            out_specs=VMEM,
            name="project",
        )(tokens, rel_table, w_query, w_key)
        received = lax.all_to_all(send, "req", 0, 0)
        if shard_rows % 16 == 0:
            table = received
        else:
            table = received[:, :shard_rows].reshape(1, req_size * shard_rows, 2 * cols)
        packed_rows = rows_dev * (width // LANES)
        parts = pl.pallas_call(
            attend_kernel,
            out_shape=jax.ShapeDtypeStruct(
                (req_size * tp_size, packed_rows, LANES), jnp.float32
            ),
            in_specs=[SMEM, SMEM] + [VMEM] * 6,
            out_specs=VMEM,
            scratch_shapes=[
                pltpu.VMEM((BUCKETS, cols), jnp.bfloat16),
                pltpu.VMEM((BUCKETS, cols), jnp.bfloat16),
                pltpu.VMEM((8, MAXLEN), jnp.float32),
                pltpu.VMEM((rows_dev, width), jnp.float32),
            ],
            name="attend",
        )(slot_of, cache_len, table, received, rel_bucket, key_cache, value_cache, w_out)
        parts = lax.all_to_all(parts, ("req", "tp"), 0, 0)
        return pl.pallas_call(
            finish_kernel,
            out_shape=jax.ShapeDtypeStruct((rows_dev, cols), jnp.bfloat16),
            in_specs=[SMEM] + [VMEM] * 4,
            out_specs=VMEM,
            scratch_shapes=[
                pltpu.VMEM((packed_rows, LANES), jnp.float32),
                pltpu.VMEM((width // LANES, LANES), jnp.float32),
                pltpu.VMEM((rows_dev, cols), jnp.float32),
            ],
            name="finish",
        )(slot_of, parts, tokens, out_gain.reshape(1, cols), out_bias.reshape(1, cols))

    return per_device


def solution(mesh):
    in_specs = (
        P("req", None),
        P(),
        P("req", None, "tp"),
        P("req", None, "tp"),
        P("req"),
        P("req", None),
        P("req", None),
        P(None, "tp"),
        P(None, "tp"),
        P("tp", None),
        P("tp"),
        P("tp"),
    )
    return jax.shard_map(
        make_per_device(mesh.shape["req"], mesh.shape["tp"]),
        mesh=mesh,
        in_specs=in_specs,
        out_specs=P("req", "tp"),
        check_vma=False,
    )
```

```python
import functools
import math

import jax
import jax.numpy as jnp
from jax import lax
from jax.experimental import pallas as pl
from jax.experimental.pallas import tpu as pltpu
from jax.sharding import PartitionSpec as P

HD = 64
BUCKETS = 512
MAXLEN = 1536
BLOCK = 512
LANES = 128
QROWS = 8

epsilon = 1e-06
masked_score = -1e30

VMEM = pl.BlockSpec(memory_space=pltpu.VMEM)
SMEM = pl.BlockSpec(memory_space=pltpu.SMEM)
ANY = pl.BlockSpec(memory_space=pl.ANY)
ROOM = pltpu.CompilerParams(vmem_limit_bytes=24 * 2**20)
NT = (((1,), (1,)), ((), ()))


def dot_f32(a, b):
    return jnp.dot(a, b, preferred_element_type=jnp.float32)


def in_hbm(array):
    return pltpu.with_memory_space_constraint(array, pltpu.HBM)


def in_vmem(array):
    return pltpu.with_memory_space_constraint(array, pltpu.VMEM)


def project_kernel(
    tokens_hbm, table_hbm, w_query_hbm, w_key_hbm, out_ref,
    tokens_ref, table_ref, w_query_ref, w_key_ref, sems,
):
    loads = [
        pltpu.make_async_copy(source, target, sems.at[index])
        for index, (source, target) in enumerate(
            (
                (table_hbm, table_ref),
                (tokens_hbm, tokens_ref),
                (w_query_hbm, w_query_ref),
                (w_key_hbm, w_key_ref),
            )
        )
    ]
    for load in loads:
        load.start()
    peers = out_ref.shape[0]
    rows, rows_dev = table_ref.shape[0], tokens_ref.shape[0]
    cols = w_query_ref.shape[1]
    chunks = cols // LANES
    query_at = out_ref.shape[1] - QROWS
    pitch = query_at // (2 * chunks)
    row_id = lax.broadcasted_iota(jnp.int32, (rows, rows), 0)
    column_id = lax.broadcasted_iota(jnp.int32, (rows, rows), 1)
    flip = jnp.where(row_id + column_id == rows - 1, 1.0, 0.0).astype(jnp.bfloat16)
    loads[0].wait()
    table = table_ref[...].astype(jnp.float32)
    centred = table - jnp.mean(table, axis=1, keepdims=True)
    variance = jnp.mean(centred * centred, axis=1, keepdims=True)
    normed = (centred * lax.rsqrt(variance + epsilon)).astype(jnp.bfloat16)
    loads[1].wait()
    loads[2].wait()
    rel_query = dot_f32(normed, w_query_ref[...]).astype(jnp.bfloat16)
    rel_query = dot_f32(flip, rel_query).astype(jnp.bfloat16)
    queries = dot_f32(tokens_ref[...], w_query_ref[...])
    query_rows = [
        queries[row : row + 1, chunk * LANES : (chunk + 1) * LANES]
        for row in range(rows_dev)
        for chunk in range(chunks)
    ]
    query_rows.append(jnp.zeros((QROWS - len(query_rows), LANES), jnp.float32))
    query_block = jnp.concatenate(query_rows, axis=0).astype(jnp.bfloat16)
    loads[3].wait()
    rel_key = dot_f32(normed, w_key_ref[...]).astype(jnp.bfloat16)
    for peer in range(peers):
        for chunk in range(chunks):
            lanes = slice(chunk * LANES, (chunk + 1) * LANES)
            at = chunk * pitch
            out_ref[peer, at : at + rows, :] = rel_key[:, lanes]
            at = (chunks + chunk) * pitch
            out_ref[peer, at : at + rows, :] = rel_query[:, lanes]
        out_ref[peer, query_at:, :] = query_block


def split3(value):
    high = value.astype(jnp.bfloat16)
    rest = value - high.astype(jnp.float32)
    middle = rest.astype(jnp.bfloat16)
    low = (rest - middle.astype(jnp.float32)).astype(jnp.bfloat16)
    return high, middle, low


def attend_kernel(
    slot_of_ref, cache_len_ref, table_ref, queries_ref, bucket_ref, key_hbm, value_hbm, out_ref,
    key_ref, value_ref, rel_key_ref, rel_query_ref, score_ref, key_sems, value_sem,
):
    rows_dev, cols = key_ref.shape[0], key_ref.shape[2]
    heads = cols // HD
    pairs = rows_dev * heads
    chunks = cols // LANES
    shards, shard_rows = table_ref.shape[0], BUCKETS // table_ref.shape[0]
    requests = slot_of_ref.shape[0]
    query_at = queries_ref.shape[1] - QROWS
    first_slot = lax.axis_index("req") * rows_dev

    load_keys = [
        pltpu.make_async_copy(key_hbm.at[index], key_ref.at[index], key_sems.at[index])
        for index in range(rows_dev)
    ]
    load_values = pltpu.make_async_copy(value_hbm, value_ref, value_sem)
    for load in load_keys:
        load.start()
    load_values.start()

    for shard in range(shards):
        rows = slice(shard * shard_rows, (shard + 1) * shard_rows)
        mirrored = slice((shards - 1 - shard) * shard_rows, (shards - shard) * shard_rows)
        for chunk in range(chunks):
            lanes = slice(chunk * LANES, (chunk + 1) * LANES)
            at = chunk * shard_rows
            rel_key_ref[rows, lanes] = table_ref[shard, at : at + shard_rows, :]
            at = (chunks + chunk) * shard_rows
            rel_query_ref[mirrored, lanes] = table_ref[shard, at : at + shard_rows, :]

    pair_id = lax.broadcasted_iota(jnp.int32, (pairs, cols), 0)
    head_id = lax.broadcasted_iota(jnp.int32, (pairs, cols), 1) // HD
    query_heads = jnp.zeros((pairs, cols), jnp.float32)
    query_columns = []
    for index in range(rows_dev):
        slot = first_slot + index

        def find(request, found):
            return jnp.where(slot_of_ref[request] == slot, request, found)

        request = lax.fori_loop(0, requests, find, 0, unroll=min(requests, 16))
        block = queries_ref[request // rows_dev, query_at:, :].astype(jnp.float32)
        own = block[0:chunks]
        for row in range(1, rows_dev):
            own = jnp.where(
                request % rows_dev == row, block[row * chunks : (row + 1) * chunks], own
            )
        query = jnp.concatenate([own[chunk : chunk + 1] for chunk in range(chunks)], axis=1)
        query_heads = jnp.where(pair_id == index * heads + head_id, query, query_heads)
        query_columns.append(
            jnp.concatenate(
                [
                    jnp.broadcast_to(own[chunk : chunk + 1], (LANES, LANES)).T
                    for chunk in range(chunks)
                ],
                axis=0,
            )
        )
    by_bucket = lax.dot_general(
        query_heads.astype(jnp.bfloat16), rel_key_ref[...], NT, preferred_element_type=jnp.float32
    )
    shifted = jnp.concatenate((by_bucket[:, 1:], by_bucket[:, :1]), axis=1)
    rel_query = rel_query_ref[...].astype(jnp.float32).T.astype(jnp.bfloat16)
    left = jnp.concatenate((rel_query,) + split3(shifted), axis=0)

    score_ref[...] = jnp.zeros(score_ref.shape, jnp.float32)
    table_id = lax.broadcasted_iota(jnp.int32, (BUCKETS, BLOCK), 0)
    for index in range(rows_dev):
        own_pairs = slice(index * heads, (index + 1) * heads)
        query_column = jnp.concatenate([query_columns[index]] * (BLOCK // LANES), axis=1)
        load_keys[index].wait()
        for offset in range(0, MAXLEN, BLOCK):

            def block_scores():
                here = slice(offset, offset + BLOCK)
                bucket = bucket_ref[index : index + 1, here]
                one_hot = jnp.where(table_id == jnp.maximum(bucket - 1, 0), 1.0, 0.0)
                found = dot_f32(left, one_hot.astype(jnp.bfloat16))
                keys = key_ref[index, here, :].astype(jnp.float32).T
                products = keys * (found[:cols] + query_column)
                along = found[cols : cols + pairs] + (
                    found[cols + pairs : cols + 2 * pairs] + found[cols + 2 * pairs :]
                )
                along = jnp.where(bucket == 0, by_bucket[:, 0:1], along)
                sums = [
                    jnp.sum(products[head * HD : (head + 1) * HD], axis=0, keepdims=True)
                    for head in range(heads)
                ]
                score_ref[own_pairs, here] = jnp.concatenate(sums, axis=0) + along[own_pairs]

            if offset:
                pl.when(offset < cache_len_ref[index])(block_scores)
            else:
                block_scores()

    lengths = jnp.full((pairs, 1), cache_len_ref[0], jnp.int32)
    for index in range(1, rows_dev):
        row = lax.broadcasted_iota(jnp.int32, (pairs, 1), 0)
        lengths = jnp.where(row >= index * heads, cache_len_ref[index], lengths)
    live = lax.broadcasted_iota(jnp.int32, score_ref.shape, 1) < lengths
    scores = jnp.where(live, score_ref[...] * (1.0 / math.sqrt(3.0 * HD)), masked_score)
    highest = jnp.max(scores, axis=1, keepdims=True)
    exponent = jnp.where(live, jnp.exp(scores - highest), 0.0)
    weights = (exponent / jnp.sum(exponent, axis=1, keepdims=True)).astype(jnp.bfloat16)
    load_values.wait()
    contexts = []
    for index in range(rows_dev):
        spread = dot_f32(weights, value_ref[index])
        spread = jnp.where(pair_id == index * heads + head_id, spread, 0.0)
        contexts.append(jnp.sum(spread, axis=0, keepdims=True))
    context = jnp.concatenate(contexts, axis=0).astype(jnp.bfloat16)
    out_ref[...] = jnp.broadcast_to(context[None], out_ref.shape)


def finish_kernel(tp_size, slot_of_ref, contexts_ref, tokens_ref, gain_ref, bias_ref, *refs):
    w_refs, (out_ref, norm_ref) = refs[:tp_size], refs[tp_size:]
    rows_dev, width = tokens_ref.shape
    cols = out_ref.shape[1]
    first_row = lax.axis_index("req") * rows_dev
    tp_index = lax.axis_index("tp")
    attended = tokens_ref[...].astype(jnp.float32)
    for step in range(tp_size):
        rows = []
        for row in range(rows_dev):
            slot = slot_of_ref[first_row + row]
            source = (slot // rows_dev) * tp_size + (tp_index ^ step)
            pair = contexts_ref[source].astype(jnp.float32)
            own = pair[0:1]
            for other in range(1, rows_dev):
                own = jnp.where(lax.rem(slot, rows_dev) == other, pair[other : other + 1], own)
            rows.append(own)
        context = jnp.concatenate(rows, axis=0).astype(jnp.bfloat16)
        attended = attended + dot_f32(context, w_refs[step][...])
    mean = jnp.mean(attended, axis=1, keepdims=True)
    centred = attended - mean
    variance = jnp.mean(centred * centred, axis=1, keepdims=True)
    norm_ref[...] = centred * lax.rsqrt(variance + epsilon)
    own_cols = norm_ref[:, pl.ds(pl.multiple_of(tp_index * cols, cols), cols)]
    out_ref[...] = (own_cols * gain_ref[...] + bias_ref[...]).astype(out_ref.dtype)


def gather_xor(block, tp_size):
    blocks = [block]
    bit = tp_size // 2
    held = {0: block}
    while bit:
        perm = [(i, i ^ bit) for i in range(tp_size)]
        for have in list(held):
            held[have ^ bit] = lax.ppermute(held[have], "tp", perm)
        bit //= 2
    return [held[step] for step in range(tp_size)]


def make_per_device(req_size, tp_size):
    def per_device(
        tokens,
        slot_of,
        key_cache,
        value_cache,
        cache_len,
        rel_bucket,
        rel_table,
        w_query,
        w_key,
        w_out,
        out_gain,
        out_bias,
    ):
        rows_dev, width = tokens.shape
        cols = w_query.shape[1]
        chunks = cols // LANES
        shard_rows = rel_table.shape[0]
        pitch = -(-shard_rows // 8) * 8
        table_rows = 2 * chunks * pitch
        send = pl.pallas_call(
            project_kernel,
            out_shape=jax.ShapeDtypeStruct((req_size, table_rows + QROWS, LANES), jnp.bfloat16),
            in_specs=[ANY] * 4,
            out_specs=VMEM,
            scratch_shapes=[
                pltpu.VMEM(tokens.shape, jnp.bfloat16),
                pltpu.VMEM(rel_table.shape, jnp.bfloat16),
                pltpu.VMEM(w_query.shape, jnp.bfloat16),
                pltpu.VMEM(w_key.shape, jnp.bfloat16),
                pltpu.SemaphoreType.DMA((4,)),
            ],
            name="project",
        )(*[in_hbm(array) for array in (tokens, rel_table, w_query, w_key)])
        send, w_out = lax.optimization_barrier((send, w_out))
        received = lax.all_to_all(send, "req", 0, 0)
        w_blocks = gather_xor(w_out, tp_size)
        if shard_rows % 16 == 0:
            table = received
        else:
            table = received[:, :table_rows].reshape(req_size, 2, chunks, pitch, LANES)
            table = table[:, :, :, :shard_rows]
            table = jnp.stack((table[:, 0], table[::-1, 1]), axis=0)
            table = table.transpose(0, 2, 1, 3, 4).reshape(1, -1, LANES)
        contexts = pl.pallas_call(
            attend_kernel,
            out_shape=jax.ShapeDtypeStruct((req_size * tp_size, rows_dev, cols), jnp.bfloat16),
            in_specs=[SMEM, SMEM, VMEM, VMEM, VMEM, ANY, ANY],
            out_specs=VMEM,
            scratch_shapes=[
                pltpu.VMEM(key_cache.shape, jnp.bfloat16),
                pltpu.VMEM(value_cache.shape, jnp.bfloat16),
                pltpu.VMEM((BUCKETS, cols), jnp.bfloat16),
                pltpu.VMEM((BUCKETS, cols), jnp.bfloat16),
                pltpu.VMEM((rows_dev * cols // HD, MAXLEN), jnp.float32),
                pltpu.SemaphoreType.DMA((rows_dev,)),
                pltpu.SemaphoreType.DMA,
            ],
            name="attend",
            compiler_params=ROOM,
        )(slot_of, cache_len, table, received, rel_bucket, in_hbm(key_cache), in_hbm(value_cache))
        contexts = lax.all_to_all(contexts, ("req", "tp"), 0, 0)
        return pl.pallas_call(
            functools.partial(finish_kernel, tp_size),
            out_shape=jax.ShapeDtypeStruct((rows_dev, cols), jnp.bfloat16),
            in_specs=[SMEM] + [VMEM] * (4 + tp_size),
            out_specs=VMEM,
            scratch_shapes=[pltpu.VMEM((rows_dev, width), jnp.float32)],
            name="finish",
            compiler_params=ROOM,
        )(
            slot_of,
            contexts,
            tokens,
            out_gain.reshape(1, cols),
            out_bias.reshape(1, cols),
            *[in_vmem(block) for block in w_blocks],
        )

    return per_device


def solution(mesh):
    in_specs = (
        P("req", None),
        P(),
        P("req", None, "tp"),
        P("req", None, "tp"),
        P("req"),
        P("req", None),
        P("req", None),
        P(None, "tp"),
        P(None, "tp"),
        P("tp", None),
        P("tp"),
        P("tp"),
    )
    return jax.shard_map(
        make_per_device(mesh.shape["req"], mesh.shape["tp"]),
        mesh=mesh,
        in_specs=in_specs,
        out_specs=P("req", "tp"),
        check_vma=False,
    )
```

```python
import functools
import math

import jax
import jax.numpy as jnp
from jax import lax
from jax.experimental import pallas as pl
from jax.experimental.pallas import tpu as pltpu
from jax.sharding import PartitionSpec as P

HD = 64
BUCKETS = 512
MAXLEN = 1536
BLOCK = 256
REGION = 512
LANES = 128
QROWS = 8

epsilon = 1e-06
masked_score = -1e30

VMEM = pl.BlockSpec(memory_space=pltpu.VMEM)
SMEM = pl.BlockSpec(memory_space=pltpu.SMEM)
ANY = pl.BlockSpec(memory_space=pl.ANY)
ROOM = pltpu.CompilerParams(vmem_limit_bytes=24 * 2**20)
NT = (((1,), (1,)), ((), ()))


def dot_f32(a, b):
    return jnp.dot(a, b, preferred_element_type=jnp.float32)


def in_hbm(array):
    return pltpu.with_memory_space_constraint(array, pltpu.HBM)


def in_vmem(array):
    return pltpu.with_memory_space_constraint(array, pltpu.VMEM)


def project_kernel(
    tokens_hbm, table_hbm, w_query_hbm, w_key_hbm, out_hbm,
    tokens_ref, table_ref, w_query_ref, w_key_ref, out_ref, sems, out_sems,
):
    loads = [
        pltpu.make_async_copy(source, target, sems.at[index])
        for index, (source, target) in enumerate(
            (
                (table_hbm, table_ref),
                (tokens_hbm, tokens_ref),
                (w_query_hbm, w_query_ref),
                (w_key_hbm, w_key_ref),
            )
        )
    ]
    for load in loads:
        load.start()
    peers = out_ref.shape[0]
    rows, rows_dev = table_ref.shape[0], tokens_ref.shape[0]
    cols = w_query_ref.shape[1]
    chunks = cols // LANES
    query_at = out_ref.shape[1] - QROWS
    pitch = query_at // (2 * chunks)
    row_id = lax.broadcasted_iota(jnp.int32, (rows, rows), 0)
    column_id = lax.broadcasted_iota(jnp.int32, (rows, rows), 1)
    flip = jnp.where(row_id + column_id == rows - 1, 1.0, 0.0).astype(jnp.bfloat16)
    loads[0].wait()
    table = table_ref[...].astype(jnp.float32)
    centred = table - jnp.mean(table, axis=1, keepdims=True)
    variance = jnp.mean(centred * centred, axis=1, keepdims=True)
    normed = (centred * lax.rsqrt(variance + epsilon)).astype(jnp.bfloat16)
    loads[1].wait()
    loads[2].wait()
    rel_query = dot_f32(normed, w_query_ref[...]).astype(jnp.bfloat16)
    rel_query = dot_f32(flip, rel_query).astype(jnp.bfloat16)
    queries = dot_f32(tokens_ref[...], w_query_ref[...])
    query_rows = [
        queries[row : row + 1, chunk * LANES : (chunk + 1) * LANES]
        for row in range(rows_dev)
        for chunk in range(chunks)
    ]
    query_rows.append(jnp.zeros((QROWS - len(query_rows), LANES), jnp.float32))
    query_block = jnp.concatenate(query_rows, axis=0).astype(jnp.bfloat16)
    half = chunks * pitch
    store_query = pltpu.make_async_copy(
        out_ref.at[:, pl.ds(half, half + QROWS)],
        out_hbm.at[:, pl.ds(half, half + QROWS)],
        out_sems.at[0],
    )
    store_key = pltpu.make_async_copy(
        out_ref.at[:, pl.ds(0, half)], out_hbm.at[:, pl.ds(0, half)], out_sems.at[1]
    )
    for peer in range(peers):
        for chunk in range(chunks):
            at = half + chunk * pitch
            out_ref[peer, at : at + rows, :] = rel_query[:, chunk * LANES : (chunk + 1) * LANES]
        out_ref[peer, query_at:, :] = query_block
    store_query.start()
    loads[3].wait()
    rel_key = dot_f32(normed, w_key_ref[...]).astype(jnp.bfloat16)
    for peer in range(peers):
        for chunk in range(chunks):
            at = chunk * pitch
            out_ref[peer, at : at + rows, :] = rel_key[:, chunk * LANES : (chunk + 1) * LANES]
    store_key.start()
    store_query.wait()
    store_key.wait()


def split3(value):
    high = value.astype(jnp.bfloat16)
    rest = value - high.astype(jnp.float32)
    middle = rest.astype(jnp.bfloat16)
    low = (rest - middle.astype(jnp.float32)).astype(jnp.bfloat16)
    return high, middle, low


def attend_kernel(
    slot_of_ref, cache_len_hbm, table_ref, queries_ref, bucket_ref, key_hbm, value_hbm, out_ref,
    key_ref, value_ref, rel_key_ref, rel_query_ref, score_ref, cache_len_ref,
    key_sems, value_sem, len_sem,
):
    rows_dev, cols = key_ref.shape[0], key_ref.shape[2]
    heads = cols // HD
    pairs = rows_dev * heads
    chunks = cols // LANES
    shards, shard_rows = table_ref.shape[0], BUCKETS // table_ref.shape[0]
    requests = slot_of_ref.shape[1]
    query_at = queries_ref.shape[1] - QROWS
    first_slot = lax.axis_index("req") * rows_dev

    load_keys = [
        pltpu.make_async_copy(key_hbm.at[index], key_ref.at[index], key_sems.at[index])
        for index in range(rows_dev)
    ]
    load_values = pltpu.make_async_copy(value_hbm, value_ref, value_sem)
    load_lengths = pltpu.make_async_copy(cache_len_hbm, cache_len_ref, len_sem)
    load_lengths.start()
    for load in load_keys:
        load.start()
    load_values.start()

    for shard in range(shards):
        rows = slice(shard * shard_rows, (shard + 1) * shard_rows)
        mirrored = slice((shards - 1 - shard) * shard_rows, (shards - shard) * shard_rows)
        for chunk in range(chunks):
            lanes = slice(chunk * LANES, (chunk + 1) * LANES)
            at = chunk * shard_rows
            rel_key_ref[rows, lanes] = table_ref[shard, at : at + shard_rows, :]
            at = (chunks + chunk) * shard_rows
            rel_query_ref[mirrored, lanes] = table_ref[shard, at : at + shard_rows, :]

    sources = queries_ref.shape[0]
    places = sources * QROWS
    held = rows_dev * chunks
    request_id = lax.broadcasted_iota(jnp.int32, (requests, places), 0)
    place = lax.broadcasted_iota(jnp.int32, (requests, places), 1)
    place_request = (place // QROWS) * rows_dev + (place % QROWS) // chunks
    used = (place % QROWS < held) & (place_request == request_id)
    slots = jnp.broadcast_to(slot_of_ref[...].astype(jnp.float32), (QROWS, requests))
    slot_at = dot_f32(slots.astype(jnp.bfloat16), jnp.where(used, 1.0, 0.0).astype(jnp.bfloat16))
    wanted = lax.broadcasted_iota(jnp.int32, (QROWS, places), 0)
    place = lax.broadcasted_iota(jnp.int32, (QROWS, places), 1) % QROWS
    hit = (
        (slot_at == (first_slot + wanted // chunks).astype(jnp.float32))
        & (place % chunks == wanted % chunks)
        & (place < held)
        & (wanted < held)
    )
    query_rows = jnp.concatenate(
        [queries_ref[source, query_at:, :].astype(jnp.float32) for source in range(sources)], axis=0
    )
    own_queries = dot_f32(
        jnp.where(hit, 1.0, 0.0).astype(jnp.bfloat16), query_rows.astype(jnp.bfloat16)
    )

    pair_id = lax.broadcasted_iota(jnp.int32, (pairs, cols), 0)
    head_id = lax.broadcasted_iota(jnp.int32, (pairs, cols), 1) // HD
    query_heads = jnp.zeros((pairs, cols), jnp.float32)
    query_columns = []
    for index in range(rows_dev):
        own = own_queries[index * chunks : (index + 1) * chunks]
        query = jnp.concatenate([own[chunk : chunk + 1] for chunk in range(chunks)], axis=1)
        query_heads = jnp.where(pair_id == index * heads + head_id, query, query_heads)
        query_columns.append(
            jnp.concatenate(
                [
                    jnp.broadcast_to(own[chunk : chunk + 1], (LANES, LANES)).T
                    for chunk in range(chunks)
                ],
                axis=0,
            )
        )
    by_bucket = lax.dot_general(
        query_heads.astype(jnp.bfloat16), rel_key_ref[...], NT, preferred_element_type=jnp.float32
    )
    shifted = jnp.concatenate((by_bucket[:, 1:], by_bucket[:, :1]), axis=1)
    rel_query = rel_query_ref[...].astype(jnp.float32).T.astype(jnp.bfloat16)
    left = jnp.concatenate((rel_query,) + split3(shifted), axis=0)

    score_ref[...] = jnp.zeros(score_ref.shape, jnp.float32)
    load_lengths.wait()
    table_id = lax.broadcasted_iota(jnp.int32, (BUCKETS, BLOCK), 0)
    table_half = (table_id - BUCKETS // 2).astype(jnp.bfloat16)
    for index in range(rows_dev):
        own_pairs = slice(index * heads, (index + 1) * heads)
        query_column = jnp.concatenate([query_columns[index]] * (BLOCK // LANES), axis=1)
        load_keys[index].wait()
        for region in range(0, MAXLEN, REGION):

            def region_scores():
                for offset in range(region, region + REGION, BLOCK):
                    block_scores(offset)

            def block_scores(offset):
                here = slice(offset, offset + BLOCK)
                bucket = bucket_ref[index : index + 1, here]
                one_hot = jnp.where(table_half == (jnp.maximum(bucket - 1, 0) - BUCKETS // 2).astype(jnp.bfloat16), jnp.bfloat16(1.0), jnp.bfloat16(0.0))
                found = dot_f32(left, one_hot.astype(jnp.bfloat16))
                keys = key_ref[index, here, :].astype(jnp.float32).T
                products = keys * (found[:cols] + query_column)
                along = found[cols : cols + pairs] + (
                    found[cols + pairs : cols + 2 * pairs] + found[cols + 2 * pairs :]
                )
                along = jnp.where(bucket == 0, by_bucket[:, 0:1], along)
                sums = [
                    jnp.sum(products[head * HD : (head + 1) * HD], axis=0, keepdims=True)
                    for head in range(heads)
                ]
                score_ref[own_pairs, here] = jnp.concatenate(sums, axis=0) + along[own_pairs]

            if region:
                pl.when(region < cache_len_ref[index])(region_scores)
            else:
                region_scores()

    lengths = jnp.full((pairs, 1), cache_len_ref[0], jnp.int32)
    for index in range(1, rows_dev):
        row = lax.broadcasted_iota(jnp.int32, (pairs, 1), 0)
        lengths = jnp.where(row >= index * heads, cache_len_ref[index], lengths)
    live = lax.broadcasted_iota(jnp.int32, score_ref.shape, 1) < lengths
    scores = jnp.where(live, score_ref[...] * (1.0 / math.sqrt(3.0 * HD)), masked_score)
    highest = jnp.max(scores, axis=1, keepdims=True)
    exponent = jnp.where(live, jnp.exp(scores - highest), 0.0)
    weights = (exponent / jnp.sum(exponent, axis=1, keepdims=True)).astype(jnp.bfloat16)
    load_values.wait()
    contexts = []
    for index in range(rows_dev):
        spread = dot_f32(weights, value_ref[index])
        spread = jnp.where(pair_id == index * heads + head_id, spread, 0.0)
        contexts.append(jnp.sum(spread, axis=0, keepdims=True))
    context = jnp.concatenate(contexts, axis=0).astype(jnp.bfloat16)
    out_ref[...] = jnp.broadcast_to(context[None], out_ref.shape)


def finish_kernel(tp_size, slot_of_ref, contexts_ref, tokens_ref, gain_ref, bias_ref, *refs):
    w_refs, (out_ref, norm_ref) = refs[:tp_size], refs[tp_size:]
    rows_dev, width = tokens_ref.shape
    cols = out_ref.shape[1]
    requests = slot_of_ref.shape[1]
    first_row = lax.axis_index("req") * rows_dev
    tp_index = lax.axis_index("tp")
    lane = lax.broadcasted_iota(jnp.int32, (8, requests), 1)
    row = lax.broadcasted_iota(jnp.int32, (8, requests), 0)
    slots = jnp.broadcast_to(slot_of_ref[...].astype(jnp.float32), (8, requests))
    slot = jnp.sum(jnp.where(lane == first_row + row, slots, 0.0), axis=1, keepdims=True)
    chosen = jnp.where(lane.astype(jnp.float32) == slot, 1.0, 0.0).astype(jnp.bfloat16)
    product = jnp.zeros((8, width), jnp.float32)
    for step in range(tp_size):
        context = jnp.concatenate(
            [
                contexts_ref[source * tp_size + (tp_index ^ step)].astype(jnp.float32)
                for source in range(requests // rows_dev)
            ],
            axis=0,
        )
        context = dot_f32(chosen, context.astype(jnp.bfloat16)).astype(jnp.bfloat16)
        product = product + dot_f32(context, w_refs[step][...])
    attended = product[0:rows_dev] + tokens_ref[...].astype(jnp.float32)
    mean = jnp.mean(attended, axis=1, keepdims=True)
    centred = attended - mean
    variance = jnp.mean(centred * centred, axis=1, keepdims=True)
    norm_ref[...] = centred * lax.rsqrt(variance + epsilon)
    own_cols = norm_ref[:, pl.ds(pl.multiple_of(tp_index * cols, cols), cols)]
    out_ref[...] = (own_cols * gain_ref[...] + bias_ref[...]).astype(out_ref.dtype)


def xor_permute(block, tp_size, bit):
    return lax.ppermute(block, "tp", [(i, i ^ bit) for i in range(tp_size)])


def gather_half(block, tp_size):
    return {0: block, 2: xor_permute(block, tp_size, 2), 1: xor_permute(block, tp_size, 1)}


def complete(held, tp_size):
    return [held[0], held[1], held[2], xor_permute(held[2], tp_size, 1)]


def make_per_device(req_size, tp_size):
    def per_device(
        tokens,
        slot_of,
        key_cache,
        value_cache,
        cache_len,
        rel_bucket,
        rel_table,
        w_query,
        w_key,
        w_out,
        out_gain,
        out_bias,
    ):
        rows_dev, width = tokens.shape
        slots = slot_of.reshape(1, -1)
        cols = w_query.shape[1]
        chunks = cols // LANES
        shard_rows = rel_table.shape[0]
        pitch = -(-shard_rows // 8) * 8
        table_rows = 2 * chunks * pitch
        send = pl.pallas_call(
            project_kernel,
            out_shape=jax.ShapeDtypeStruct((req_size, table_rows + QROWS, LANES), jnp.bfloat16),
            in_specs=[ANY] * 4,
            out_specs=ANY,
            scratch_shapes=[
                pltpu.VMEM(tokens.shape, jnp.bfloat16),
                pltpu.VMEM(rel_table.shape, jnp.bfloat16),
                pltpu.VMEM(w_query.shape, jnp.bfloat16),
                pltpu.VMEM(w_key.shape, jnp.bfloat16),
                pltpu.VMEM((req_size, table_rows + QROWS, LANES), jnp.bfloat16),
                pltpu.SemaphoreType.DMA((4,)),
                pltpu.SemaphoreType.DMA((2,)),
            ],
            name="project",
        )(*[in_hbm(array) for array in (tokens, rel_table, w_query, w_key)])
        send, w_out = lax.optimization_barrier((send, w_out))
        received = lax.all_to_all(send, "req", 0, 0)
        w_blocks = gather_half(w_out, tp_size)
        if shard_rows % 16 == 0:
            table = received
        else:
            table = received[:, :table_rows].reshape(req_size, 2, chunks, pitch, LANES)
            table = table[:, :, :, :shard_rows]
            table = jnp.stack((table[:, 0], table[::-1, 1]), axis=0)
            table = table.transpose(0, 2, 1, 3, 4).reshape(1, -1, LANES)
        contexts = pl.pallas_call(
            attend_kernel,
            out_shape=jax.ShapeDtypeStruct((req_size * tp_size, rows_dev, cols), jnp.bfloat16),
            in_specs=[VMEM, ANY, VMEM, VMEM, VMEM, ANY, ANY],
            out_specs=VMEM,
            scratch_shapes=[
                pltpu.VMEM(key_cache.shape, jnp.bfloat16),
                pltpu.VMEM(value_cache.shape, jnp.bfloat16),
                pltpu.VMEM((BUCKETS, cols), jnp.bfloat16),
                pltpu.VMEM((BUCKETS, cols), jnp.bfloat16),
                pltpu.VMEM((rows_dev * cols // HD, MAXLEN), jnp.float32),
                pltpu.SMEM((rows_dev,), jnp.int32),
                pltpu.SemaphoreType.DMA((rows_dev,)),
                pltpu.SemaphoreType.DMA,
                pltpu.SemaphoreType.DMA,
            ],
            name="attend",
            cost_estimate=pl.CostEstimate(flops=20_000_000_000, transcendentals=0, bytes_accessed=30_000_000),
            compiler_params=ROOM,
        )(slots, in_hbm(cache_len), table, received, rel_bucket, in_hbm(key_cache), in_hbm(value_cache))
        contexts, w_blocks = lax.optimization_barrier((contexts, w_blocks))
        w_blocks = complete(w_blocks, tp_size)
        contexts = lax.all_to_all(contexts, ("req", "tp"), 0, 0)
        return pl.pallas_call(
            functools.partial(finish_kernel, tp_size),
            out_shape=jax.ShapeDtypeStruct((rows_dev, cols), jnp.bfloat16),
            in_specs=[VMEM] * (5 + tp_size),
            out_specs=VMEM,
            scratch_shapes=[pltpu.VMEM((rows_dev, width), jnp.float32)],
            name="finish",
            compiler_params=ROOM,
        )(
            slots,
            contexts,
            tokens,
            out_gain.reshape(1, cols),
            out_bias.reshape(1, cols),
            *[in_vmem(block) for block in w_blocks],
        )

    return per_device


def solution(mesh):
    in_specs = (
        P("req", None),
        P(),
        P("req", None, "tp"),
        P("req", None, "tp"),
        P("req"),
        P("req", None),
        P("req", None),
        P(None, "tp"),
        P(None, "tp"),
        P("tp", None),
        P("tp"),
        P("tp"),
    )
    return jax.shard_map(
        make_per_device(mesh.shape["req"], mesh.shape["tp"]),
        mesh=mesh,
        in_specs=in_specs,
        out_specs=P("req", "tp"),
        check_vma=False,
    )
```

```python
import functools
import math

import jax
import jax.numpy as jnp
from jax import lax
from jax.experimental import pallas as pl
from jax.experimental.pallas import tpu as pltpu
from jax.sharding import PartitionSpec as P

HD = 64
BUCKETS = 512
MAXLEN = 1536
BLOCK = 256
REGION = 512
LANES = 128
QROWS = 8

epsilon = 1e-06
masked_score = -1e30

VMEM = pl.BlockSpec(memory_space=pltpu.VMEM)
SMEM = pl.BlockSpec(memory_space=pltpu.SMEM)
ANY = pl.BlockSpec(memory_space=pl.ANY)
ROOM = pltpu.CompilerParams(vmem_limit_bytes=24 * 2**20)
NT = (((1,), (1,)), ((), ()))


def dot_f32(a, b):
    return jnp.dot(a, b, preferred_element_type=jnp.float32)


def in_hbm(array):
    return pltpu.with_memory_space_constraint(array, pltpu.HBM)


def in_vmem(array):
    return pltpu.with_memory_space_constraint(array, pltpu.VMEM)


def project_kernel(
    tokens_hbm, table_hbm, w_query_hbm, w_key_hbm, out_ref,
    tokens_ref, table_ref, w_query_ref, w_key_ref, sems,
):
    loads = [
        pltpu.make_async_copy(source, target, sems.at[index])
        for index, (source, target) in enumerate(
            (
                (table_hbm, table_ref),
                (tokens_hbm, tokens_ref),
                (w_query_hbm, w_query_ref),
                (w_key_hbm, w_key_ref),
            )
        )
    ]
    for load in loads:
        load.start()
    rows, rows_dev = table_ref.shape[0], tokens_ref.shape[0]
    cols = w_query_ref.shape[1]
    chunks = cols // LANES
    query_at = out_ref.shape[0] - QROWS
    pitch = query_at // (2 * chunks)
    row_id = lax.broadcasted_iota(jnp.int32, (rows, rows), 0)
    column_id = lax.broadcasted_iota(jnp.int32, (rows, rows), 1)
    flip = jnp.where(row_id + column_id == rows - 1, 1.0, 0.0).astype(jnp.bfloat16)
    loads[0].wait()
    table = table_ref[...].astype(jnp.float32)
    centred = table - jnp.mean(table, axis=1, keepdims=True)
    variance = jnp.mean(centred * centred, axis=1, keepdims=True)
    normed = (centred * lax.rsqrt(variance + epsilon)).astype(jnp.bfloat16)
    loads[1].wait()
    loads[2].wait()
    rel_query = dot_f32(normed, w_query_ref[...]).astype(jnp.bfloat16)
    rel_query = dot_f32(flip, rel_query).astype(jnp.bfloat16)
    queries = dot_f32(tokens_ref[...], w_query_ref[...])
    query_rows = [
        queries[row : row + 1, chunk * LANES : (chunk + 1) * LANES]
        for row in range(rows_dev)
        for chunk in range(chunks)
    ]
    query_rows.append(jnp.zeros((QROWS - len(query_rows), LANES), jnp.float32))
    query_block = jnp.concatenate(query_rows, axis=0).astype(jnp.bfloat16)
    for chunk in range(chunks):
        at = (chunks + chunk) * pitch
        out_ref[at : at + rows, :] = rel_query[:, chunk * LANES : (chunk + 1) * LANES]
    out_ref[query_at:, :] = query_block
    loads[3].wait()
    rel_key = dot_f32(normed, w_key_ref[...]).astype(jnp.bfloat16)
    for chunk in range(chunks):
        at = chunk * pitch
        out_ref[at : at + rows, :] = rel_key[:, chunk * LANES : (chunk + 1) * LANES]


def spread_kernel(own_ref, mirror_ref, out_ref):
    rows = own_ref.shape[0]
    own, mirror = own_ref[...], mirror_ref[...]
    for peer in range(out_ref.shape[0]):
        out_ref[peer, 0:rows, :] = own
        out_ref[peer, rows : 2 * rows, :] = mirror


def split3(value):
    high = value.astype(jnp.bfloat16)
    rest = value - high.astype(jnp.float32)
    middle = rest.astype(jnp.bfloat16)
    low = (rest - middle.astype(jnp.float32)).astype(jnp.bfloat16)
    return high, middle, low


def attend_kernel(
    by_halves, slot_of_ref, cache_len_hbm, table_ref, queries_ref, bucket_ref, key_hbm, value_hbm, out_ref,
    key_ref, value_ref, rel_key_ref, rel_query_ref, score_ref, cache_len_ref,
    key_sems, value_sem, len_sem,
):
    rows_dev, cols = key_ref.shape[0], key_ref.shape[2]
    heads = cols // HD
    pairs = rows_dev * heads
    chunks = cols // LANES
    shards, shard_rows = table_ref.shape[0], BUCKETS // table_ref.shape[0]
    requests = slot_of_ref.shape[1]
    query_at = queries_ref.shape[1] - QROWS
    first_slot = lax.axis_index("req") * rows_dev

    load_keys = [
        pltpu.make_async_copy(key_hbm.at[index], key_ref.at[index], key_sems.at[index])
        for index in range(rows_dev)
    ]
    load_values = pltpu.make_async_copy(value_hbm, value_ref, value_sem)
    load_lengths = pltpu.make_async_copy(cache_len_hbm, cache_len_ref, len_sem)
    load_lengths.start()
    for load in load_keys:
        load.start()
    load_values.start()

    sources = queries_ref.shape[0]
    own_half = lax.axis_index("req") // (sources // 2)

    def shard_of(source):
        if not by_halves:
            return source
        return (own_half ^ (source % 2)) * (sources // 2) + source // 2

    for source in range(shards):
        shard = shard_of(source)
        rows = pl.ds(shard * shard_rows, shard_rows)
        reversed_rows = pl.ds((shards - 1 - shard) * shard_rows, shard_rows)
        if by_halves:
            rows = pl.ds(pl.multiple_of(rows.start, shard_rows), shard_rows)
            reversed_rows = pl.ds(pl.multiple_of(reversed_rows.start, shard_rows), shard_rows)
        for chunk in range(chunks):
            lanes = slice(chunk * LANES, (chunk + 1) * LANES)
            at = chunk * shard_rows
            rel_key_ref[rows, lanes] = table_ref[source, at : at + shard_rows, :]
            at = (chunks + chunk) * shard_rows
            rel_query_ref[reversed_rows, lanes] = table_ref[source, at : at + shard_rows, :]

    places = sources * QROWS
    held = rows_dev * chunks
    request_id = lax.broadcasted_iota(jnp.int32, (requests, places), 0)
    place = lax.broadcasted_iota(jnp.int32, (requests, places), 1)
    place_request = shard_of(place // QROWS) * rows_dev + (place % QROWS) // chunks
    used = (place % QROWS < held) & (place_request == request_id)
    slots = jnp.broadcast_to(slot_of_ref[...].astype(jnp.float32), (QROWS, requests))
    slot_at = dot_f32(slots.astype(jnp.bfloat16), jnp.where(used, 1.0, 0.0).astype(jnp.bfloat16))
    wanted = lax.broadcasted_iota(jnp.int32, (QROWS, places), 0)
    place = lax.broadcasted_iota(jnp.int32, (QROWS, places), 1) % QROWS
    hit = (
        (slot_at == (first_slot + wanted // chunks).astype(jnp.float32))
        & (place % chunks == wanted % chunks)
        & (place < held)
        & (wanted < held)
    )
    query_rows = jnp.concatenate(
        [queries_ref[source, query_at:, :].astype(jnp.float32) for source in range(sources)], axis=0
    )
    own_queries = dot_f32(
        jnp.where(hit, 1.0, 0.0).astype(jnp.bfloat16), query_rows.astype(jnp.bfloat16)
    )

    pair_id = lax.broadcasted_iota(jnp.int32, (pairs, cols), 0)
    head_id = lax.broadcasted_iota(jnp.int32, (pairs, cols), 1) // HD
    query_heads = jnp.zeros((pairs, cols), jnp.float32)
    query_columns = []
    for index in range(rows_dev):
        own = own_queries[index * chunks : (index + 1) * chunks]
        query = jnp.concatenate([own[chunk : chunk + 1] for chunk in range(chunks)], axis=1)
        query_heads = jnp.where(pair_id == index * heads + head_id, query, query_heads)
        query_columns.append(
            jnp.concatenate(
                [
                    jnp.broadcast_to(own[chunk : chunk + 1], (LANES, LANES)).T
                    for chunk in range(chunks)
                ],
                axis=0,
            )
        )
    by_bucket = lax.dot_general(
        query_heads.astype(jnp.bfloat16), rel_key_ref[...], NT, preferred_element_type=jnp.float32
    )
    shifted = jnp.concatenate((by_bucket[:, 1:], by_bucket[:, :1]), axis=1)
    rel_query = rel_query_ref[...].astype(jnp.float32).T.astype(jnp.bfloat16)
    left = jnp.concatenate((rel_query,) + split3(shifted), axis=0)

    score_ref[...] = jnp.zeros(score_ref.shape, jnp.float32)
    load_lengths.wait()
    table_id = lax.broadcasted_iota(jnp.int32, (BUCKETS, BLOCK), 0)
    table_half = (table_id - BUCKETS // 2).astype(jnp.bfloat16)
    for index in range(rows_dev):
        own_pairs = slice(index * heads, (index + 1) * heads)
        query_column = jnp.concatenate([query_columns[index]] * (BLOCK // LANES), axis=1)
        load_keys[index].wait()
        for region in range(0, MAXLEN, REGION):

            def region_scores():
                for offset in range(region, region + REGION, BLOCK):
                    block_scores(offset)

            def block_scores(offset):
                here = slice(offset, offset + BLOCK)
                bucket = bucket_ref[index : index + 1, here]
                one_hot = jnp.where(table_half == (jnp.maximum(bucket - 1, 0) - BUCKETS // 2).astype(jnp.bfloat16), jnp.bfloat16(1.0), jnp.bfloat16(0.0))
                found = dot_f32(left, one_hot.astype(jnp.bfloat16))
                keys = key_ref[index, here, :].astype(jnp.float32).T
                products = keys * (found[:cols] + query_column)
                along = found[cols : cols + pairs] + (
                    found[cols + pairs : cols + 2 * pairs] + found[cols + 2 * pairs :]
                )
                along = jnp.where(bucket == 0, by_bucket[:, 0:1], along)
                sums = [
                    jnp.sum(products[head * HD : (head + 1) * HD], axis=0, keepdims=True)
                    for head in range(heads)
                ]
                score_ref[own_pairs, here] = jnp.concatenate(sums, axis=0) + along[own_pairs]

            if region:
                pl.when(region < cache_len_ref[index])(region_scores)
            else:
                region_scores()

    lengths = jnp.full((pairs, 1), cache_len_ref[0], jnp.int32)
    for index in range(1, rows_dev):
        row = lax.broadcasted_iota(jnp.int32, (pairs, 1), 0)
        lengths = jnp.where(row >= index * heads, cache_len_ref[index], lengths)
    live = lax.broadcasted_iota(jnp.int32, score_ref.shape, 1) < lengths
    scores = jnp.where(live, score_ref[...] * (1.0 / math.sqrt(3.0 * HD)), masked_score)
    highest = jnp.max(scores, axis=1, keepdims=True)
    exponent = jnp.where(live, jnp.exp(scores - highest), 0.0)
    weights = (exponent / jnp.sum(exponent, axis=1, keepdims=True)).astype(jnp.bfloat16)
    load_values.wait()
    contexts = []
    for index in range(rows_dev):
        spread = dot_f32(weights, value_ref[index])
        spread = jnp.where(pair_id == index * heads + head_id, spread, 0.0)
        contexts.append(jnp.sum(spread, axis=0, keepdims=True))
    context = jnp.concatenate(contexts, axis=0).astype(jnp.bfloat16)
    out_ref[...] = jnp.broadcast_to(context[None], out_ref.shape)


def finish_kernel(tp_size, slot_of_ref, contexts_ref, tokens_ref, gain_ref, bias_ref, *refs):
    w_refs, (out_ref, norm_ref) = refs[:tp_size], refs[tp_size:]
    rows_dev, width = tokens_ref.shape
    cols = out_ref.shape[1]
    requests = slot_of_ref.shape[1]
    first_row = lax.axis_index("req") * rows_dev
    tp_index = lax.axis_index("tp")
    lane = lax.broadcasted_iota(jnp.int32, (8, requests), 1)
    row = lax.broadcasted_iota(jnp.int32, (8, requests), 0)
    slots = jnp.broadcast_to(slot_of_ref[...].astype(jnp.float32), (8, requests))
    slot = jnp.sum(jnp.where(lane == first_row + row, slots, 0.0), axis=1, keepdims=True)
    chosen = jnp.where(lane.astype(jnp.float32) == slot, 1.0, 0.0).astype(jnp.bfloat16)
    product = jnp.zeros((8, width), jnp.float32)
    for step in range(tp_size):
        context = jnp.concatenate(
            [
                contexts_ref[source * tp_size + (tp_index ^ step)].astype(jnp.float32)
                for source in range(requests // rows_dev)
            ],
            axis=0,
        )
        context = dot_f32(chosen, context.astype(jnp.bfloat16)).astype(jnp.bfloat16)
        product = product + dot_f32(context, w_refs[step][...])
    attended = product[0:rows_dev] + tokens_ref[...].astype(jnp.float32)
    mean = jnp.mean(attended, axis=1, keepdims=True)
    centred = attended - mean
    variance = jnp.mean(centred * centred, axis=1, keepdims=True)
    norm_ref[...] = centred * lax.rsqrt(variance + epsilon)
    own_cols = norm_ref[:, pl.ds(pl.multiple_of(tp_index * cols, cols), cols)]
    out_ref[...] = (own_cols * gain_ref[...] + bias_ref[...]).astype(out_ref.dtype)


def xor_permute(block, tp_size, bit):
    return lax.ppermute(block, "tp", [(i, i ^ bit) for i in range(tp_size)])


def gather_half(block, tp_size):
    return {0: block, 2: xor_permute(block, tp_size, 2), 1: xor_permute(block, tp_size, 1)}


def complete(held, tp_size):
    return [held[0], held[1], held[2], xor_permute(held[2], tp_size, 1)]


def make_per_device(req_size, tp_size):
    def per_device(
        tokens,
        slot_of,
        key_cache,
        value_cache,
        cache_len,
        rel_bucket,
        rel_table,
        w_query,
        w_key,
        w_out,
        out_gain,
        out_bias,
    ):
        rows_dev, width = tokens.shape
        slots = slot_of.reshape(1, -1)
        cols = w_query.shape[1]
        chunks = cols // LANES
        shard_rows = rel_table.shape[0]
        pitch = -(-shard_rows // 8) * 8
        table_rows = 2 * chunks * pitch
        block_rows = table_rows + QROWS
        block = pl.pallas_call(
            project_kernel,
            out_shape=jax.ShapeDtypeStruct((block_rows, LANES), jnp.bfloat16),
            in_specs=[ANY] * 4,
            out_specs=VMEM,
            scratch_shapes=[
                pltpu.VMEM(tokens.shape, jnp.bfloat16),
                pltpu.VMEM(rel_table.shape, jnp.bfloat16),
                pltpu.VMEM(w_query.shape, jnp.bfloat16),
                pltpu.VMEM(w_key.shape, jnp.bfloat16),
                pltpu.SemaphoreType.DMA((4,)),
            ],
            name="project",
            compiler_params=ROOM,
        )(*[in_hbm(array) for array in (tokens, rel_table, w_query, w_key)])
        half = req_size // 2
        mirror = lax.ppermute(block, "req", [(i, (i + half) % req_size) for i in range(req_size)])
        send = pl.pallas_call(
            spread_kernel,
            out_shape=jax.ShapeDtypeStruct((half, 2 * block_rows, LANES), jnp.bfloat16),
            in_specs=[VMEM] * 2,
            out_specs=VMEM,
            name="spread",
            compiler_params=ROOM,
        )(block, mirror)
        halves = [list(range(half)), list(range(half, req_size))]
        received = lax.all_to_all(send, "req", 0, 0, axis_index_groups=halves)
        w_blocks = gather_half(lax.optimization_barrier((block, w_out))[1], tp_size)
        received = received.reshape(req_size, block_rows, LANES)
        by_halves = shard_rows % 16 == 0
        if by_halves:
            table = received
        else:
            received = received.reshape(half, 2, block_rows, LANES).transpose(1, 0, 2, 3)
            first = lax.axis_index("req") < half
            received = jnp.where(first, received, received[::-1])
            received = received.reshape(req_size, block_rows, LANES)
            table = received[:, :table_rows].reshape(req_size, 2, chunks, pitch, LANES)
            table = table[:, :, :, :shard_rows]
            table = jnp.stack((table[:, 0], table[::-1, 1]), axis=0)
            table = table.transpose(0, 2, 1, 3, 4).reshape(1, -1, LANES)
        contexts = pl.pallas_call(
            functools.partial(attend_kernel, by_halves),
            out_shape=jax.ShapeDtypeStruct((req_size * tp_size, rows_dev, cols), jnp.bfloat16),
            in_specs=[VMEM, ANY, VMEM, VMEM, VMEM, ANY, ANY],
            out_specs=VMEM,
            scratch_shapes=[
                pltpu.VMEM(key_cache.shape, jnp.bfloat16),
                pltpu.VMEM(value_cache.shape, jnp.bfloat16),
                pltpu.VMEM((BUCKETS, cols), jnp.bfloat16),
                pltpu.VMEM((BUCKETS, cols), jnp.bfloat16),
                pltpu.VMEM((rows_dev * cols // HD, MAXLEN), jnp.float32),
                pltpu.SMEM((rows_dev,), jnp.int32),
                pltpu.SemaphoreType.DMA((rows_dev,)),
                pltpu.SemaphoreType.DMA,
                pltpu.SemaphoreType.DMA,
            ],
            name="attend",
            compiler_params=ROOM,
        )(slots, in_hbm(cache_len), table, received, rel_bucket, in_hbm(key_cache), in_hbm(value_cache))
        contexts, w_blocks = lax.optimization_barrier((contexts, complete(w_blocks, tp_size)))
        contexts = lax.all_to_all(contexts, ("req", "tp"), 0, 0)
        return pl.pallas_call(
            functools.partial(finish_kernel, tp_size),
            out_shape=jax.ShapeDtypeStruct((rows_dev, cols), jnp.bfloat16),
            in_specs=[VMEM] * (5 + tp_size),
            out_specs=VMEM,
            scratch_shapes=[pltpu.VMEM((rows_dev, width), jnp.float32)],
            name="finish",
            compiler_params=ROOM,
        )(
            slots,
            contexts,
            tokens,
            out_gain.reshape(1, cols),
            out_bias.reshape(1, cols),
            *[in_vmem(block) for block in w_blocks],
        )

    return per_device


def solution(mesh):
    in_specs = (
        P("req", None),
        P(),
        P("req", None, "tp"),
        P("req", None, "tp"),
        P("req"),
        P("req", None),
        P("req", None),
        P(None, "tp"),
        P(None, "tp"),
        P("tp", None),
        P("tp"),
        P("tp"),
    )
    return jax.shard_map(
        make_per_device(mesh.shape["req"], mesh.shape["tp"]),
        mesh=mesh,
        in_specs=in_specs,
        out_specs=P("req", "tp"),
        check_vma=False,
    )
```

```python
import functools
import math

import jax
import jax.numpy as jnp
from jax import lax
from jax.experimental import pallas as pl
from jax.experimental.pallas import tpu as pltpu
from jax.sharding import PartitionSpec as P

HD = 64
BUCKETS = 512
MAXLEN = 1536
BLOCK = 256
REGION = 512
LANES = 128
QROWS = 8

epsilon = 1e-06
masked_score = -1e30

VMEM = pl.BlockSpec(memory_space=pltpu.VMEM)
SMEM = pl.BlockSpec(memory_space=pltpu.SMEM)
ANY = pl.BlockSpec(memory_space=pl.ANY)
ROOM = pltpu.CompilerParams(vmem_limit_bytes=24 * 2**20)
NT = (((1,), (1,)), ((), ()))


def dot_f32(a, b):
    return jnp.dot(a, b, preferred_element_type=jnp.float32)


def in_hbm(array):
    return pltpu.with_memory_space_constraint(array, pltpu.HBM)


def in_vmem(array):
    return pltpu.with_memory_space_constraint(array, pltpu.VMEM)


def project_kernel(
    tokens_hbm, table_hbm, w_query_hbm, w_key_hbm, out_ref,
    tokens_ref, table_ref, w_query_ref, w_key_ref, sems,
):
    loads = [
        pltpu.make_async_copy(source, target, sems.at[index])
        for index, (source, target) in enumerate(
            (
                (table_hbm, table_ref),
                (tokens_hbm, tokens_ref),
                (w_query_hbm, w_query_ref),
                (w_key_hbm, w_key_ref),
            )
        )
    ]
    for load in loads:
        load.start()
    rows, rows_dev = table_ref.shape[0], tokens_ref.shape[0]
    cols = w_query_ref.shape[1]
    chunks = cols // LANES
    query_at = out_ref.shape[0] - QROWS
    pitch = query_at // (2 * chunks)
    row_id = lax.broadcasted_iota(jnp.int32, (rows, rows), 0)
    column_id = lax.broadcasted_iota(jnp.int32, (rows, rows), 1)
    flip = jnp.where(row_id + column_id == rows - 1, 1.0, 0.0).astype(jnp.bfloat16)
    loads[0].wait()
    table = table_ref[...].astype(jnp.float32)
    centred = table - jnp.mean(table, axis=1, keepdims=True)
    variance = jnp.mean(centred * centred, axis=1, keepdims=True)
    normed = (centred * lax.rsqrt(variance + epsilon)).astype(jnp.bfloat16)
    loads[1].wait()
    loads[2].wait()
    rel_query = dot_f32(normed, w_query_ref[...]).astype(jnp.bfloat16)
    rel_query = dot_f32(flip, rel_query).astype(jnp.bfloat16)
    queries = dot_f32(tokens_ref[...], w_query_ref[...])
    query_rows = [
        queries[row : row + 1, chunk * LANES : (chunk + 1) * LANES]
        for row in range(rows_dev)
        for chunk in range(chunks)
    ]
    query_rows.append(jnp.zeros((QROWS - len(query_rows), LANES), jnp.float32))
    query_block = jnp.concatenate(query_rows, axis=0).astype(jnp.bfloat16)
    for chunk in range(chunks):
        at = (chunks + chunk) * pitch
        out_ref[at : at + rows, :] = rel_query[:, chunk * LANES : (chunk + 1) * LANES]
    out_ref[query_at:, :] = query_block
    loads[3].wait()
    rel_key = dot_f32(normed, w_key_ref[...]).astype(jnp.bfloat16)
    for chunk in range(chunks):
        at = chunk * pitch
        out_ref[at : at + rows, :] = rel_key[:, chunk * LANES : (chunk + 1) * LANES]


def spread_kernel(own_ref, mirror_ref, out_ref):
    rows = own_ref.shape[0]
    own, mirror = own_ref[...], mirror_ref[...]
    for peer in range(out_ref.shape[0]):
        out_ref[peer, 0:rows, :] = own
        out_ref[peer, rows : 2 * rows, :] = mirror


def split3(value):
    high = value.astype(jnp.bfloat16)
    rest = value - high.astype(jnp.float32)
    middle = rest.astype(jnp.bfloat16)
    low = (rest - middle.astype(jnp.float32)).astype(jnp.bfloat16)
    return high, middle, low


def attend_kernel(
    by_halves, slot_of_ref, cache_len_hbm, table_ref, queries_ref, bucket_ref, first_key_ref, key_hbm, value_hbm,
    out_ref, key_ref, value_ref, rel_key_ref, rel_query_ref, score_ref, cache_len_ref,
    key_sems, value_sem, len_sem,
):
    rows_dev, cols = key_ref.shape[0], key_ref.shape[2]
    heads = cols // HD
    pairs = rows_dev * heads
    chunks = cols // LANES
    shards, shard_rows = table_ref.shape[0], BUCKETS // table_ref.shape[0]
    requests = slot_of_ref.shape[1]
    query_at = queries_ref.shape[1] - QROWS
    first_slot = lax.axis_index("req") * rows_dev

    load_keys = [
        pltpu.make_async_copy(key_hbm.at[index], key_ref.at[index], key_sems.at[index])
        for index in range(1, rows_dev)
    ]
    load_values = pltpu.make_async_copy(value_hbm, value_ref, value_sem)
    load_lengths = pltpu.make_async_copy(cache_len_hbm, cache_len_ref, len_sem)
    load_lengths.start()
    for load in load_keys:
        load.start()
    load_values.start()

    sources = queries_ref.shape[0]
    own_half = lax.axis_index("req") // (sources // 2)

    def shard_of(source):
        if not by_halves:
            return source
        return (own_half ^ (source % 2)) * (sources // 2) + source // 2

    for source in range(shards):
        shard = shard_of(source)
        rows = pl.ds(shard * shard_rows, shard_rows)
        reversed_rows = pl.ds((shards - 1 - shard) * shard_rows, shard_rows)
        if by_halves:
            rows = pl.ds(pl.multiple_of(rows.start, shard_rows), shard_rows)
            reversed_rows = pl.ds(pl.multiple_of(reversed_rows.start, shard_rows), shard_rows)
        for chunk in range(chunks):
            lanes = slice(chunk * LANES, (chunk + 1) * LANES)
            at = chunk * shard_rows
            rel_key_ref[rows, lanes] = table_ref[source, at : at + shard_rows, :]
            at = (chunks + chunk) * shard_rows
            rel_query_ref[reversed_rows, lanes] = table_ref[source, at : at + shard_rows, :]

    places = sources * QROWS
    held = rows_dev * chunks
    request_id = lax.broadcasted_iota(jnp.int32, (requests, places), 0)
    place = lax.broadcasted_iota(jnp.int32, (requests, places), 1)
    place_request = shard_of(place // QROWS) * rows_dev + (place % QROWS) // chunks
    used = (place % QROWS < held) & (place_request == request_id)
    slots = jnp.broadcast_to(slot_of_ref[...].astype(jnp.float32), (QROWS, requests))
    slot_at = dot_f32(slots.astype(jnp.bfloat16), jnp.where(used, 1.0, 0.0).astype(jnp.bfloat16))
    wanted = lax.broadcasted_iota(jnp.int32, (QROWS, places), 0)
    place = lax.broadcasted_iota(jnp.int32, (QROWS, places), 1) % QROWS
    hit = (
        (slot_at == (first_slot + wanted // chunks).astype(jnp.float32))
        & (place % chunks == wanted % chunks)
        & (place < held)
        & (wanted < held)
    )
    query_rows = jnp.concatenate(
        [queries_ref[source, query_at:, :].astype(jnp.float32) for source in range(sources)], axis=0
    )
    own_queries = dot_f32(
        jnp.where(hit, 1.0, 0.0).astype(jnp.bfloat16), query_rows.astype(jnp.bfloat16)
    )

    pair_id = lax.broadcasted_iota(jnp.int32, (pairs, cols), 0)
    head_id = lax.broadcasted_iota(jnp.int32, (pairs, cols), 1) // HD
    query_heads = jnp.zeros((pairs, cols), jnp.float32)
    query_columns = []
    for index in range(rows_dev):
        own = own_queries[index * chunks : (index + 1) * chunks]
        query = jnp.concatenate([own[chunk : chunk + 1] for chunk in range(chunks)], axis=1)
        query_heads = jnp.where(pair_id == index * heads + head_id, query, query_heads)
        query_columns.append(
            jnp.concatenate(
                [
                    jnp.broadcast_to(own[chunk : chunk + 1], (LANES, LANES)).T
                    for chunk in range(chunks)
                ],
                axis=0,
            )
        )
    by_bucket = lax.dot_general(
        query_heads.astype(jnp.bfloat16), rel_key_ref[...], NT, preferred_element_type=jnp.float32
    )
    shifted = jnp.concatenate((by_bucket[:, 1:], by_bucket[:, :1]), axis=1)
    rel_query = rel_query_ref[...].astype(jnp.float32).T.astype(jnp.bfloat16)
    left = jnp.concatenate((rel_query,) + split3(shifted), axis=0)

    score_ref[...] = jnp.zeros(score_ref.shape, jnp.float32)
    load_lengths.wait()
    table_id = lax.broadcasted_iota(jnp.int32, (BUCKETS, BLOCK), 0)
    table_half = (table_id - BUCKETS // 2).astype(jnp.bfloat16)
    for index in range(rows_dev):
        own_pairs = slice(index * heads, (index + 1) * heads)
        query_column = jnp.concatenate([query_columns[index]] * (BLOCK // LANES), axis=1)
        if index:
            load_keys[index - 1].wait()
        for region in range(0, MAXLEN, REGION):

            def region_scores():
                for offset in range(region, region + REGION, BLOCK):
                    block_scores(offset)

            def block_scores(offset):
                here = slice(offset, offset + BLOCK)
                bucket = bucket_ref[index : index + 1, here]
                one_hot = jnp.where(table_half == (jnp.maximum(bucket - 1, 0) - BUCKETS // 2).astype(jnp.bfloat16), jnp.bfloat16(1.0), jnp.bfloat16(0.0))
                found = dot_f32(left, one_hot.astype(jnp.bfloat16))
                keys = key_ref[index, here, :] if index else first_key_ref[here, :]
                keys = keys.astype(jnp.float32).T
                products = keys * (found[:cols] + query_column)
                along = found[cols : cols + pairs] + (
                    found[cols + pairs : cols + 2 * pairs] + found[cols + 2 * pairs :]
                )
                along = jnp.where(bucket == 0, by_bucket[:, 0:1], along)
                sums = [
                    jnp.sum(products[head * HD : (head + 1) * HD], axis=0, keepdims=True)
                    for head in range(heads)
                ]
                score_ref[own_pairs, here] = jnp.concatenate(sums, axis=0) + along[own_pairs]

            if region:
                pl.when(region < cache_len_ref[index])(region_scores)
            else:
                region_scores()

    lengths = jnp.full((pairs, 1), cache_len_ref[0], jnp.int32)
    for index in range(1, rows_dev):
        row = lax.broadcasted_iota(jnp.int32, (pairs, 1), 0)
        lengths = jnp.where(row >= index * heads, cache_len_ref[index], lengths)
    live = lax.broadcasted_iota(jnp.int32, score_ref.shape, 1) < lengths
    scores = jnp.where(live, score_ref[...] * (1.0 / math.sqrt(3.0 * HD)), masked_score)
    highest = jnp.max(scores, axis=1, keepdims=True)
    exponent = jnp.where(live, jnp.exp(scores - highest), 0.0)
    weights = (exponent / jnp.sum(exponent, axis=1, keepdims=True)).astype(jnp.bfloat16)
    load_values.wait()
    contexts = []
    for index in range(rows_dev):
        spread = dot_f32(weights, value_ref[index])
        spread = jnp.where(pair_id == index * heads + head_id, spread, 0.0)
        contexts.append(jnp.sum(spread, axis=0, keepdims=True))
    context = jnp.concatenate(contexts, axis=0).astype(jnp.bfloat16)
    out_ref[...] = jnp.broadcast_to(context[None], out_ref.shape)


def finish_kernel(tp_size, slot_of_ref, contexts_ref, tokens_ref, gain_ref, bias_ref, *refs):
    w_refs, (out_ref, norm_ref) = refs[:tp_size], refs[tp_size:]
    rows_dev, width = tokens_ref.shape
    cols = out_ref.shape[1]
    requests = slot_of_ref.shape[1]
    first_row = lax.axis_index("req") * rows_dev
    tp_index = lax.axis_index("tp")
    lane = lax.broadcasted_iota(jnp.int32, (8, requests), 1)
    row = lax.broadcasted_iota(jnp.int32, (8, requests), 0)
    slots = jnp.broadcast_to(slot_of_ref[...].astype(jnp.float32), (8, requests))
    slot = jnp.sum(jnp.where(lane == first_row + row, slots, 0.0), axis=1, keepdims=True)
    chosen = jnp.where(lane.astype(jnp.float32) == slot, 1.0, 0.0).astype(jnp.bfloat16)
    products = []
    gathered = jnp.concatenate(
        [
            jnp.concatenate(
                [
                    contexts_ref[source * tp_size + (tp_index ^ step)].astype(jnp.float32)
                    for source in range(requests // rows_dev)
                ],
                axis=0,
            )
            for step in range(tp_size)
        ],
        axis=1,
    )
    context = dot_f32(chosen, gathered.astype(jnp.bfloat16)).astype(jnp.bfloat16)
    for step in range(tp_size):
        products.append(dot_f32(context[:, step * cols : (step + 1) * cols], w_refs[step][...]))
    while len(products) > 1:
        products = [a + b for a, b in zip(products[::2], products[1::2], strict=True)]
    product = products[0]
    attended = product[0:rows_dev] + tokens_ref[...].astype(jnp.float32)
    mean = jnp.mean(attended, axis=1, keepdims=True)
    centred = attended - mean
    variance = jnp.mean(centred * centred, axis=1, keepdims=True)
    norm_ref[...] = centred * lax.rsqrt(variance + epsilon)
    own_cols = norm_ref[:, pl.ds(pl.multiple_of(tp_index * cols, cols), cols)]
    out_ref[...] = (own_cols * gain_ref[...] + bias_ref[...]).astype(out_ref.dtype)


def xor_permute(block, tp_size, bit):
    return lax.ppermute(block, "tp", [(i, i ^ bit) for i in range(tp_size)])


def gather_half(block, tp_size):
    return {0: block, 2: xor_permute(block, tp_size, 2), 1: xor_permute(block, tp_size, 1)}


def complete(held, tp_size):
    return [held[0], held[1], held[2], xor_permute(held[2], tp_size, 1)]


def make_per_device(req_size, tp_size):
    def per_device(
        tokens,
        slot_of,
        key_cache,
        value_cache,
        cache_len,
        rel_bucket,
        rel_table,
        w_query,
        w_key,
        w_out,
        out_gain,
        out_bias,
    ):
        rows_dev, width = tokens.shape
        slots = slot_of.reshape(1, -1)
        cols = w_query.shape[1]
        chunks = cols // LANES
        shard_rows = rel_table.shape[0]
        pitch = -(-shard_rows // 8) * 8
        table_rows = 2 * chunks * pitch
        block_rows = table_rows + QROWS
        block = pl.pallas_call(
            project_kernel,
            out_shape=jax.ShapeDtypeStruct((block_rows, LANES), jnp.bfloat16),
            in_specs=[ANY] * 4,
            out_specs=VMEM,
            scratch_shapes=[
                pltpu.VMEM(tokens.shape, jnp.bfloat16),
                pltpu.VMEM(rel_table.shape, jnp.bfloat16),
                pltpu.VMEM(w_query.shape, jnp.bfloat16),
                pltpu.VMEM(w_key.shape, jnp.bfloat16),
                pltpu.SemaphoreType.DMA((4,)),
            ],
            name="project",
            compiler_params=ROOM,
        )(*[in_hbm(array) for array in (tokens, rel_table, w_query, w_key)])
        half = req_size // 2
        mirror = lax.ppermute(block, "req", [(i, (i + half) % req_size) for i in range(req_size)])
        send = pl.pallas_call(
            spread_kernel,
            out_shape=jax.ShapeDtypeStruct((half, 2 * block_rows, LANES), jnp.bfloat16),
            in_specs=[VMEM] * 2,
            out_specs=VMEM,
            name="spread",
            compiler_params=ROOM,
        )(block, mirror)
        halves = [list(range(half)), list(range(half, req_size))]
        received = lax.all_to_all(send, "req", 0, 0, axis_index_groups=halves)
        w_blocks = gather_half(lax.optimization_barrier((block, w_out))[1], tp_size)
        received = received.reshape(req_size, block_rows, LANES)
        by_halves = shard_rows % 16 == 0
        if by_halves:
            table = received
        else:
            received = received.reshape(half, 2, block_rows, LANES).transpose(1, 0, 2, 3)
            first = lax.axis_index("req") < half
            received = jnp.where(first, received, received[::-1])
            received = received.reshape(req_size, block_rows, LANES)
            table = received[:, :table_rows].reshape(req_size, 2, chunks, pitch, LANES)
            table = table[:, :, :, :shard_rows]
            table = jnp.stack((table[:, 0], table[::-1, 1]), axis=0)
            table = table.transpose(0, 2, 1, 3, 4).reshape(1, -1, LANES)
        contexts = pl.pallas_call(
            functools.partial(attend_kernel, by_halves),
            out_shape=jax.ShapeDtypeStruct((req_size * tp_size, rows_dev, cols), jnp.bfloat16),
            in_specs=[VMEM, ANY] + [VMEM] * 4 + [ANY, ANY],
            out_specs=VMEM,
            scratch_shapes=[
                pltpu.VMEM(key_cache.shape, jnp.bfloat16),
                pltpu.VMEM(value_cache.shape, jnp.bfloat16),
                pltpu.VMEM((BUCKETS, cols), jnp.bfloat16),
                pltpu.VMEM((BUCKETS, cols), jnp.bfloat16),
                pltpu.VMEM((rows_dev * cols // HD, MAXLEN), jnp.float32),
                pltpu.SMEM((rows_dev,), jnp.int32),
                pltpu.SemaphoreType.DMA((rows_dev,)),
                pltpu.SemaphoreType.DMA,
                pltpu.SemaphoreType.DMA,
            ],
            name="attend",
            compiler_params=ROOM,
        )(
            slots,
            in_hbm(cache_len),
            table,
            received,
            rel_bucket,
            in_vmem(key_cache[0]),
            in_hbm(key_cache),
            in_hbm(value_cache),
        )
        contexts, w_blocks = lax.optimization_barrier((contexts, complete(w_blocks, tp_size)))
        contexts = lax.all_to_all(contexts, ("req", "tp"), 0, 0)
        return pl.pallas_call(
            functools.partial(finish_kernel, tp_size),
            out_shape=jax.ShapeDtypeStruct((rows_dev, cols), jnp.bfloat16),
            in_specs=[VMEM] * (5 + tp_size),
            out_specs=VMEM,
            scratch_shapes=[pltpu.VMEM((rows_dev, width), jnp.float32)],
            name="finish",
            compiler_params=ROOM,
        )(
            slots,
            contexts,
            tokens,
            out_gain.reshape(1, cols),
            out_bias.reshape(1, cols),
            *[in_vmem(block) for block in w_blocks],
        )

    return per_device


def solution(mesh):
    in_specs = (
        P("req", None),
        P(),
        P("req", None, "tp"),
        P("req", None, "tp"),
        P("req"),
        P("req", None),
        P("req", None),
        P(None, "tp"),
        P(None, "tp"),
        P("tp", None),
        P("tp"),
        P("tp"),
    )
    return jax.shard_map(
        make_per_device(mesh.shape["req"], mesh.shape["tp"]),
        mesh=mesh,
        in_specs=in_specs,
        out_specs=P("req", "tp"),
        check_vma=False,
    )
```

```python
import functools
import itertools
import math

import jax
import jax.numpy as jnp
from jax import lax
from jax.experimental import pallas as pl
from jax.experimental.pallas import tpu as pltpu
from jax.sharding import PartitionSpec as P

HD = 64
BUCKETS = 512
MAXLEN = 1536
BLOCK = 256
REGION = 512
LANES = 128
QROWS = 8

epsilon = 1e-06
masked_score = -1e30

VMEM = pl.BlockSpec(memory_space=pltpu.VMEM)
SMEM = pl.BlockSpec(memory_space=pltpu.SMEM)
ANY = pl.BlockSpec(memory_space=pl.ANY)
ROOM = pltpu.CompilerParams(vmem_limit_bytes=24 * 2**20)
NT = (((1,), (1,)), ((), ()))


def dot_f32(a, b):
    return jnp.dot(a, b, preferred_element_type=jnp.float32)


def in_hbm(array):
    return pltpu.with_memory_space_constraint(array, pltpu.HBM)


def in_vmem(array):
    return pltpu.with_memory_space_constraint(array, pltpu.VMEM)


def project_kernel(
    tokens_hbm, table_hbm, w_query_hbm, w_key_hbm, out_ref,
    tokens_ref, table_ref, w_query_ref, w_key_ref, sems,
):
    loads = [
        pltpu.make_async_copy(source, target, sems.at[index])
        for index, (source, target) in enumerate(
            (
                (table_hbm, table_ref),
                (tokens_hbm, tokens_ref),
                (w_query_hbm, w_query_ref),
                (w_key_hbm, w_key_ref),
            )
        )
    ]
    for load in loads:
        load.start()
    rows, rows_dev = table_ref.shape[0], tokens_ref.shape[0]
    cols = w_query_ref.shape[1]
    chunks = cols // LANES
    query_at = out_ref.shape[0] - QROWS
    pitch = query_at // (2 * chunks)
    row_id = lax.broadcasted_iota(jnp.int32, (rows, rows), 0)
    column_id = lax.broadcasted_iota(jnp.int32, (rows, rows), 1)
    flip = jnp.where(row_id + column_id == rows - 1, 1.0, 0.0).astype(jnp.bfloat16)
    loads[0].wait()
    table = table_ref[...].astype(jnp.float32)
    centred = table - jnp.mean(table, axis=1, keepdims=True)
    variance = jnp.mean(centred * centred, axis=1, keepdims=True)
    normed = (centred * lax.rsqrt(variance + epsilon)).astype(jnp.bfloat16)
    loads[1].wait()
    loads[2].wait()
    rel_query = dot_f32(normed, w_query_ref[...]).astype(jnp.bfloat16)
    rel_query = dot_f32(flip, rel_query).astype(jnp.bfloat16)
    queries = dot_f32(tokens_ref[...], w_query_ref[...])
    query_rows = [
        queries[row : row + 1, chunk * LANES : (chunk + 1) * LANES]
        for row in range(rows_dev)
        for chunk in range(chunks)
    ]
    query_rows.append(jnp.zeros((QROWS - len(query_rows), LANES), jnp.float32))
    query_block = jnp.concatenate(query_rows, axis=0).astype(jnp.bfloat16)
    for chunk in range(chunks):
        at = (chunks + chunk) * pitch
        out_ref[at : at + rows, :] = rel_query[:, chunk * LANES : (chunk + 1) * LANES]
    out_ref[query_at:, :] = query_block
    loads[3].wait()
    rel_key = dot_f32(normed, w_key_ref[...]).astype(jnp.bfloat16)
    for chunk in range(chunks):
        at = chunk * pitch
        out_ref[at : at + rows, :] = rel_key[:, chunk * LANES : (chunk + 1) * LANES]


def spread_kernel(own_ref, mirror_ref, out_ref):
    rows = own_ref.shape[0]
    own, mirror = own_ref[...], mirror_ref[...]
    for peer in range(out_ref.shape[0]):
        out_ref[peer, 0:rows, :] = own
        out_ref[peer, rows : 2 * rows, :] = mirror


def split3(value):
    high = value.astype(jnp.bfloat16)
    rest = value - high.astype(jnp.float32)
    middle = rest.astype(jnp.bfloat16)
    low = (rest - middle.astype(jnp.float32)).astype(jnp.bfloat16)
    return high, middle, low


def attend_kernel(
    by_halves, slot_of_ref, cache_len_ref, table_ref, queries_ref, bucket_ref, first_key_ref, key_hbm, value_hbm,
    out_ref, key_ref, value_ref, rel_key_ref, rel_query_ref, score_ref, key_sems, value_sems,
):
    rows_dev, cols = key_ref.shape[0], key_ref.shape[2]
    heads = cols // HD
    pairs = rows_dev * heads
    chunks = cols // LANES
    shards, shard_rows = table_ref.shape[0], BUCKETS // table_ref.shape[0]
    requests = slot_of_ref.shape[1]
    query_at = queries_ref.shape[1] - QROWS
    first_slot = lax.axis_index("req") * rows_dev

    def load(source, target, sems, index, part):
        rows = pl.ds(0, REGION) if part == 0 else pl.ds(REGION, MAXLEN - REGION)
        return pltpu.make_async_copy(
            source.at[index, rows], target.at[index, rows], sems.at[index, part]
        )

    load_keys = functools.partial(load, key_hbm, key_ref, key_sems)
    load_values = functools.partial(load, value_hbm, value_ref, value_sems)

    def start_loads(index, part):
        if index:
            load_keys(index, part).start()
        load_values(index, part).start()

    for index in reversed(range(rows_dev)):
        start_loads(index, 0)
    lane = lax.broadcasted_iota(jnp.int32, (1, rows_dev), 1)
    cache_len = cache_len_ref[...].astype(jnp.float32)
    is_long = [
        jnp.sum(jnp.where(lane == index, cache_len, 0.0)) > REGION for index in range(rows_dev)
    ]
    for index in reversed(range(rows_dev)):

        @pl.when(is_long[index])
        def _():
            start_loads(index, 1)

    sources = queries_ref.shape[0]
    own_half = lax.axis_index("req") // (sources // 2)

    def shard_of(source):
        if not by_halves:
            return source
        return (own_half ^ (source % 2)) * (sources // 2) + source // 2

    for source in range(shards):
        shard = shard_of(source)
        rows = pl.ds(shard * shard_rows, shard_rows)
        reversed_rows = pl.ds((shards - 1 - shard) * shard_rows, shard_rows)
        if by_halves:
            rows = pl.ds(pl.multiple_of(rows.start, shard_rows), shard_rows)
            reversed_rows = pl.ds(pl.multiple_of(reversed_rows.start, shard_rows), shard_rows)
        for chunk in range(chunks):
            lanes = slice(chunk * LANES, (chunk + 1) * LANES)
            at = chunk * shard_rows
            rel_key_ref[rows, lanes] = table_ref[source, at : at + shard_rows, :]
            at = (chunks + chunk) * shard_rows
            rel_query_ref[reversed_rows, lanes] = table_ref[source, at : at + shard_rows, :]

    places = sources * QROWS
    held = rows_dev * chunks
    request_id = lax.broadcasted_iota(jnp.int32, (requests, places), 0)
    place = lax.broadcasted_iota(jnp.int32, (requests, places), 1)
    place_request = shard_of(place // QROWS) * rows_dev + (place % QROWS) // chunks
    used = (place % QROWS < held) & (place_request == request_id)
    slots = jnp.broadcast_to(slot_of_ref[...].astype(jnp.float32), (QROWS, requests))
    slot_at = dot_f32(slots.astype(jnp.bfloat16), jnp.where(used, 1.0, 0.0).astype(jnp.bfloat16))
    wanted = lax.broadcasted_iota(jnp.int32, (QROWS, places), 0)
    place = lax.broadcasted_iota(jnp.int32, (QROWS, places), 1) % QROWS
    hit = (
        (slot_at == (first_slot + wanted // chunks).astype(jnp.float32))
        & (place % chunks == wanted % chunks)
        & (place < held)
        & (wanted < held)
    )
    query_rows = jnp.concatenate(
        [queries_ref[source, query_at:, :].astype(jnp.float32) for source in range(sources)], axis=0
    )
    own_queries = dot_f32(
        jnp.where(hit, 1.0, 0.0).astype(jnp.bfloat16), query_rows.astype(jnp.bfloat16)
    )

    pair_id = lax.broadcasted_iota(jnp.int32, (pairs, cols), 0)
    head_id = lax.broadcasted_iota(jnp.int32, (pairs, cols), 1) // HD
    query_heads = jnp.zeros((pairs, cols), jnp.float32)
    query_columns = []
    for index in range(rows_dev):
        own = own_queries[index * chunks : (index + 1) * chunks]
        query = jnp.concatenate([own[chunk : chunk + 1] for chunk in range(chunks)], axis=1)
        query_heads = jnp.where(pair_id == index * heads + head_id, query, query_heads)
        query_columns.append(
            jnp.concatenate(
                [
                    jnp.broadcast_to(own[chunk : chunk + 1], (LANES, LANES)).T
                    for chunk in range(chunks)
                ],
                axis=0,
            )
        )
    by_bucket = lax.dot_general(
        query_heads.astype(jnp.bfloat16), rel_key_ref[...], NT, preferred_element_type=jnp.float32
    )
    shifted = jnp.concatenate((by_bucket[:, 1:], by_bucket[:, :1]), axis=1)
    rel_query = rel_query_ref[...].astype(jnp.float32).T.astype(jnp.bfloat16)
    left = jnp.concatenate((rel_query,) + split3(shifted), axis=0)

    pair_row = lax.broadcasted_iota(jnp.int32, (pairs, rows_dev), 0) // heads
    pair_column = lax.broadcasted_iota(jnp.int32, (pairs, rows_dev), 1)
    lengths = jnp.sum(jnp.where(pair_row == pair_column, cache_len, 0.0), axis=1, keepdims=True)
    table_id = lax.broadcasted_iota(jnp.int32, (BUCKETS, BLOCK), 0)
    table_half = (table_id - BUCKETS // 2).astype(jnp.bfloat16)

    def block_scores(index, offset):
        here = slice(offset, offset + BLOCK)
        bucket = bucket_ref[index : index + 1, here]
        row = (jnp.maximum(bucket - 1, 0) - BUCKETS // 2).astype(jnp.bfloat16)
        one_hot = jnp.where(table_half == row, jnp.bfloat16(1.0), jnp.bfloat16(0.0))
        found = dot_f32(left, one_hot)
        keys = key_ref[index, here, :] if index else first_key_ref[here, :]
        query_column = jnp.concatenate([query_columns[index]] * (BLOCK // LANES), axis=1)
        products = keys.astype(jnp.float32).T * (found[:cols] + query_column)
        along = found[cols : cols + pairs] + (
            found[cols + pairs : cols + 2 * pairs] + found[cols + 2 * pairs :]
        )
        along = jnp.where(bucket == 0, by_bucket[:, 0:1], along)
        sums = [
            jnp.sum(products[head * HD : (head + 1) * HD], axis=0, keepdims=True)
            for head in range(heads)
        ]
        own_pairs = slice(index * heads, (index + 1) * heads)
        score_ref[own_pairs, here] = jnp.concatenate(sums, axis=0) + along[own_pairs]

    def attend(sizes):
        width = max(sizes)
        for index in range(rows_dev):
            own_pairs = slice(index * heads, (index + 1) * heads)
            if sizes[index] < width:
                score_ref[own_pairs, sizes[index] : width] = jnp.zeros(
                    (heads, width - sizes[index]), jnp.float32
                )
            for offset in range(0, sizes[index], BLOCK):
                if index and offset in (0, REGION):
                    load_keys(index, offset // REGION).wait()
                block_scores(index, offset)
        place = lax.broadcasted_iota(jnp.int32, (pairs, width), 1)
        live = place.astype(jnp.float32) < lengths
        scores = score_ref[:, 0:width] * (1.0 / math.sqrt(3.0 * HD))
        scores = jnp.where(live, scores, masked_score)
        highest = jnp.max(scores, axis=1, keepdims=True)
        exponent = jnp.where(live, jnp.exp(scores - highest), 0.0)
        weights = (exponent / jnp.sum(exponent, axis=1, keepdims=True)).astype(jnp.bfloat16)
        contexts = []
        for index in reversed(range(rows_dev)):
            size = sizes[index]
            for part in range(1 if size == REGION else 2):
                load_values(index, part).wait()
            spread = dot_f32(weights[:, 0:size], value_ref[index, 0:size, :])
            spread = jnp.where(pair_id == index * heads + head_id, spread, 0.0)
            contexts.append(jnp.sum(spread, axis=0, keepdims=True))
        context = jnp.concatenate(contexts[::-1], axis=0).astype(jnp.bfloat16)
        out_ref[...] = jnp.broadcast_to(context[None], out_ref.shape)

    for case in itertools.product((False, True), repeat=rows_dev):
        taken = [is_long[index] == case[index] for index in range(rows_dev)]
        sizes = [MAXLEN if long else REGION for long in case]
        pl.when(functools.reduce(jnp.logical_and, taken))(functools.partial(attend, sizes))


def finish_kernel(tp_size, slot_of_ref, contexts_ref, tokens_ref, gain_ref, bias_ref, *refs):
    w_refs, (out_ref, norm_ref) = refs[:tp_size], refs[tp_size:]
    rows_dev, width = tokens_ref.shape
    cols = out_ref.shape[1]
    requests = slot_of_ref.shape[1]
    first_row = lax.axis_index("req") * rows_dev
    tp_index = lax.axis_index("tp")
    lane = lax.broadcasted_iota(jnp.int32, (8, requests), 1)
    row = lax.broadcasted_iota(jnp.int32, (8, requests), 0)
    slots = jnp.broadcast_to(slot_of_ref[...].astype(jnp.float32), (8, requests))
    slot = jnp.sum(jnp.where(lane == first_row + row, slots, 0.0), axis=1, keepdims=True)
    chosen = jnp.where(lane.astype(jnp.float32) == slot, 1.0, 0.0).astype(jnp.bfloat16)
    products = []
    gathered = jnp.concatenate(
        [
            jnp.concatenate(
                [
                    contexts_ref[source * tp_size + (tp_index ^ step)].astype(jnp.float32)
                    for source in range(requests // rows_dev)
                ],
                axis=0,
            )
            for step in range(tp_size)
        ],
        axis=1,
    )
    context = dot_f32(chosen, gathered.astype(jnp.bfloat16)).astype(jnp.bfloat16)
    for step in range(tp_size):
        products.append(dot_f32(context[:, step * cols : (step + 1) * cols], w_refs[step][...]))
    while len(products) > 1:
        products = [a + b for a, b in zip(products[::2], products[1::2], strict=True)]
    product = products[0]
    attended = product[0:rows_dev] + tokens_ref[...].astype(jnp.float32)
    mean = jnp.mean(attended, axis=1, keepdims=True)
    centred = attended - mean
    variance = jnp.mean(centred * centred, axis=1, keepdims=True)
    norm_ref[...] = centred * lax.rsqrt(variance + epsilon)
    own_cols = norm_ref[:, pl.ds(pl.multiple_of(tp_index * cols, cols), cols)]
    out_ref[...] = (own_cols * gain_ref[...] + bias_ref[...]).astype(out_ref.dtype)


def xor_permute(block, tp_size, bit):
    return lax.ppermute(block, "tp", [(i, i ^ bit) for i in range(tp_size)])


def gather_half(block, tp_size):
    return {0: block, 2: xor_permute(block, tp_size, 2), 1: xor_permute(block, tp_size, 1)}


def complete(held, tp_size):
    return [held[0], held[1], held[2], xor_permute(held[2], tp_size, 1)]


def make_per_device(req_size, tp_size):
    def per_device(
        tokens,
        slot_of,
        key_cache,
        value_cache,
        cache_len,
        rel_bucket,
        rel_table,
        w_query,
        w_key,
        w_out,
        out_gain,
        out_bias,
    ):
        rows_dev, width = tokens.shape
        slots = slot_of.reshape(1, -1)
        cols = w_query.shape[1]
        chunks = cols // LANES
        shard_rows = rel_table.shape[0]
        pitch = -(-shard_rows // 8) * 8
        table_rows = 2 * chunks * pitch
        block_rows = table_rows + QROWS
        block = pl.pallas_call(
            project_kernel,
            out_shape=jax.ShapeDtypeStruct((block_rows, LANES), jnp.bfloat16),
            in_specs=[ANY] * 4,
            out_specs=VMEM,
            scratch_shapes=[
                pltpu.VMEM(tokens.shape, jnp.bfloat16),
                pltpu.VMEM(rel_table.shape, jnp.bfloat16),
                pltpu.VMEM(w_query.shape, jnp.bfloat16),
                pltpu.VMEM(w_key.shape, jnp.bfloat16),
                pltpu.SemaphoreType.DMA((4,)),
            ],
            name="project",
            compiler_params=ROOM,
        )(*[in_hbm(array) for array in (tokens, rel_table, w_query, w_key)])
        half = req_size // 2
        mirror = lax.ppermute(block, "req", [(i, (i + half) % req_size) for i in range(req_size)])
        send = pl.pallas_call(
            spread_kernel,
            out_shape=jax.ShapeDtypeStruct((half, 2 * block_rows, LANES), jnp.bfloat16),
            in_specs=[VMEM] * 2,
            out_specs=VMEM,
            name="spread",
            compiler_params=ROOM,
        )(block, mirror)
        halves = [list(range(half)), list(range(half, req_size))]
        received = lax.all_to_all(send, "req", 0, 0, axis_index_groups=halves)
        w_blocks = gather_half(lax.optimization_barrier((block, w_out))[1], tp_size)
        received = received.reshape(req_size, block_rows, LANES)
        by_halves = shard_rows % 16 == 0
        if by_halves:
            table = received
        else:
            received = received.reshape(half, 2, block_rows, LANES).transpose(1, 0, 2, 3)
            first = lax.axis_index("req") < half
            received = jnp.where(first, received, received[::-1])
            received = received.reshape(req_size, block_rows, LANES)
            table = received[:, :table_rows].reshape(req_size, 2, chunks, pitch, LANES)
            table = table[:, :, :, :shard_rows]
            table = jnp.stack((table[:, 0], table[::-1, 1]), axis=0)
            table = table.transpose(0, 2, 1, 3, 4).reshape(1, -1, LANES)
        contexts = pl.pallas_call(
            functools.partial(attend_kernel, by_halves),
            out_shape=jax.ShapeDtypeStruct((req_size * tp_size, rows_dev, cols), jnp.bfloat16),
            in_specs=[VMEM] * 6 + [ANY, ANY],
            out_specs=VMEM,
            scratch_shapes=[
                pltpu.VMEM(key_cache.shape, jnp.bfloat16),
                pltpu.VMEM(value_cache.shape, jnp.bfloat16),
                pltpu.VMEM((BUCKETS, cols), jnp.bfloat16),
                pltpu.VMEM((BUCKETS, cols), jnp.bfloat16),
                pltpu.VMEM((rows_dev * cols // HD, MAXLEN), jnp.float32),
                pltpu.SemaphoreType.DMA((rows_dev, 2)),
                pltpu.SemaphoreType.DMA((rows_dev, 2)),
            ],
            name="attend",
            compiler_params=ROOM,
        )(
            slots,
            cache_len.reshape(1, rows_dev),
            table,
            received,
            rel_bucket,
            in_vmem(key_cache[0]),
            in_hbm(key_cache),
            in_hbm(value_cache),
        )
        contexts, w_blocks = lax.optimization_barrier((contexts, complete(w_blocks, tp_size)))
        contexts = lax.all_to_all(contexts, ("req", "tp"), 0, 0)
        return pl.pallas_call(
            functools.partial(finish_kernel, tp_size),
            out_shape=jax.ShapeDtypeStruct((rows_dev, cols), jnp.bfloat16),
            in_specs=[VMEM] * (5 + tp_size),
            out_specs=VMEM,
            scratch_shapes=[pltpu.VMEM((rows_dev, width), jnp.float32)],
            name="finish",
            compiler_params=ROOM,
        )(
            slots,
            contexts,
            tokens,
            out_gain.reshape(1, cols),
            out_bias.reshape(1, cols),
            *[in_vmem(block) for block in w_blocks],
        )

    return per_device


def solution(mesh):
    in_specs = (
        P("req", None),
        P(),
        P("req", None, "tp"),
        P("req", None, "tp"),
        P("req"),
        P("req", None),
        P("req", None),
        P(None, "tp"),
        P(None, "tp"),
        P("tp", None),
        P("tp"),
        P("tp"),
    )
    return jax.shard_map(
        make_per_device(mesh.shape["req"], mesh.shape["tp"]),
        mesh=mesh,
        in_specs=in_specs,
        out_specs=P("req", "tp"),
        check_vma=False,
    )
```

```python
import functools
import itertools
import math

import jax
import jax.numpy as jnp
from jax import lax
from jax.experimental import pallas as pl
from jax.experimental.pallas import tpu as pltpu
from jax.sharding import PartitionSpec as P

HD = 64
BUCKETS = 512
MAXLEN = 1536
BLOCK = 256
REGION = 512
LANES = 128
QROWS = 8

epsilon = 1e-06
masked_score = -1e30

VMEM = pl.BlockSpec(memory_space=pltpu.VMEM)
SMEM = pl.BlockSpec(memory_space=pltpu.SMEM)
ANY = pl.BlockSpec(memory_space=pl.ANY)
ROOM = pltpu.CompilerParams(vmem_limit_bytes=24 * 2**20)
NT = (((1,), (1,)), ((), ()))


def dot_f32(a, b):
    return jnp.dot(a, b, preferred_element_type=jnp.float32)


def in_hbm(array):
    return pltpu.with_memory_space_constraint(array, pltpu.HBM)


def in_vmem(array):
    return pltpu.with_memory_space_constraint(array, pltpu.VMEM)


def project_kernel(
    tokens_hbm, table_hbm, w_query_hbm, w_key_hbm, out_ref,
    tokens_ref, table_ref, w_query_ref, w_key_ref, sems,
):
    loads = [
        pltpu.make_async_copy(source, target, sems.at[index])
        for index, (source, target) in enumerate(
            (
                (table_hbm, table_ref),
                (tokens_hbm, tokens_ref),
                (w_query_hbm, w_query_ref),
                (w_key_hbm, w_key_ref),
            )
        )
    ]
    for load in loads:
        load.start()
    rows, rows_dev = table_ref.shape[0], tokens_ref.shape[0]
    cols = w_query_ref.shape[1]
    chunks = cols // LANES
    query_at = out_ref.shape[0] - QROWS
    pitch = query_at // (2 * chunks)
    row_id = lax.broadcasted_iota(jnp.int32, (rows, rows), 0)
    column_id = lax.broadcasted_iota(jnp.int32, (rows, rows), 1)
    flip = jnp.where(row_id + column_id == rows - 1, 1.0, 0.0).astype(jnp.bfloat16)
    loads[0].wait()
    table = table_ref[...].astype(jnp.float32)
    centred = table - jnp.mean(table, axis=1, keepdims=True)
    variance = jnp.mean(centred * centred, axis=1, keepdims=True)
    normed = (centred * lax.rsqrt(variance + epsilon)).astype(jnp.bfloat16)
    loads[1].wait()
    loads[2].wait()
    rel_query = dot_f32(normed, w_query_ref[...]).astype(jnp.bfloat16)
    rel_query = dot_f32(flip, rel_query).astype(jnp.bfloat16)
    queries = dot_f32(tokens_ref[...], w_query_ref[...])
    query_rows = [
        queries[row : row + 1, chunk * LANES : (chunk + 1) * LANES]
        for row in range(rows_dev)
        for chunk in range(chunks)
    ]
    query_rows.append(jnp.zeros((QROWS - len(query_rows), LANES), jnp.float32))
    query_block = jnp.concatenate(query_rows, axis=0).astype(jnp.bfloat16)
    for chunk in range(chunks):
        at = (chunks + chunk) * pitch
        out_ref[at : at + rows, :] = rel_query[:, chunk * LANES : (chunk + 1) * LANES]
    out_ref[query_at:, :] = query_block
    loads[3].wait()
    rel_key = dot_f32(normed, w_key_ref[...]).astype(jnp.bfloat16)
    for chunk in range(chunks):
        at = chunk * pitch
        out_ref[at : at + rows, :] = rel_key[:, chunk * LANES : (chunk + 1) * LANES]


def longest_first(cache_len_ref):
    rows_dev = cache_len_ref.shape[1]
    lane = lax.broadcasted_iota(jnp.int32, (1, rows_dev), 1)
    cache_len = cache_len_ref[...].astype(jnp.float32)
    lengths = [jnp.sum(jnp.where(lane == slot, cache_len, 0.0)) for slot in range(rows_dev)]
    longest, first = lengths[0], jnp.int32(0)
    for slot in range(1, rows_dev):
        first = jnp.where(lengths[slot] > longest, slot, first)
        longest = jnp.maximum(lengths[slot], longest)
    order, ordered = [first], [longest]
    for place in range(1, rows_dev):
        order.append(jnp.where(first < place, place, place - 1))
        ordered.append(jnp.where(first < place, lengths[place], lengths[place - 1]))
    return order, ordered


def keep_kernel(cache_len_ref, key_hbm, out_ref, sem):
    order, _ = longest_first(cache_len_ref)
    load = pltpu.make_async_copy(key_hbm.at[order[0]], out_ref, sem)
    load.start()
    load.wait()


def spread_kernel(own_ref, mirror_ref, out_ref):
    rows = own_ref.shape[0]
    own, mirror = own_ref[...], mirror_ref[...]
    for peer in range(out_ref.shape[0]):
        out_ref[peer, 0:rows, :] = own
        out_ref[peer, rows : 2 * rows, :] = mirror


def split3(value):
    high = value.astype(jnp.bfloat16)
    rest = value - high.astype(jnp.float32)
    middle = rest.astype(jnp.bfloat16)
    low = (rest - middle.astype(jnp.float32)).astype(jnp.bfloat16)
    return high, middle, low


def attend_kernel(
    by_halves, slot_of_ref, cache_len_ref, table_ref, queries_ref, bucket_ref, first_key_ref, key_hbm, value_hbm,
    out_ref, key_ref, value_ref, rel_key_ref, rel_query_ref, score_ref, key_sems, value_sems,
):
    rows_dev, cols = key_ref.shape[0], key_ref.shape[2]
    heads = cols // HD
    pairs = rows_dev * heads
    chunks = cols // LANES
    shards, shard_rows = table_ref.shape[0], BUCKETS // table_ref.shape[0]
    requests = slot_of_ref.shape[1]
    query_at = queries_ref.shape[1] - QROWS
    first_slot = lax.axis_index("req") * rows_dev

    order, lengths = longest_first(cache_len_ref)

    def load(source, target, sems, place, part):
        rows = pl.ds(part * REGION, REGION)
        return pltpu.make_async_copy(
            source.at[order[place], rows], target.at[place, rows], sems.at[place, part]
        )

    load_keys = functools.partial(load, key_hbm, key_ref, key_sems)
    load_values = functools.partial(load, value_hbm, value_ref, value_sems)
    parts = MAXLEN // REGION

    def start_loads(place, part):
        if place:
            load_keys(place, part).start()
        load_values(place, part).start()

    for place in reversed(range(rows_dev)):
        start_loads(place, 0)

    @pl.when(lengths[0] > REGION)
    def _():
        for part in range(1, parts):
            start_loads(0, part)

    for place in range(1, rows_dev):
        for part in range(1, parts):

            @pl.when(lengths[place] > part * REGION)
            def _():
                start_loads(place, part)

    sources = queries_ref.shape[0]
    own_half = lax.axis_index("req") // (sources // 2)

    def shard_of(source):
        if not by_halves:
            return source
        return (own_half ^ (source % 2)) * (sources // 2) + source // 2

    for source in range(shards):
        shard = shard_of(source)
        rows = pl.ds(shard * shard_rows, shard_rows)
        reversed_rows = pl.ds((shards - 1 - shard) * shard_rows, shard_rows)
        if by_halves:
            rows = pl.ds(pl.multiple_of(rows.start, shard_rows), shard_rows)
            reversed_rows = pl.ds(pl.multiple_of(reversed_rows.start, shard_rows), shard_rows)
        for chunk in range(chunks):
            lanes = slice(chunk * LANES, (chunk + 1) * LANES)
            at = chunk * shard_rows
            rel_key_ref[rows, lanes] = table_ref[source, at : at + shard_rows, :]
            at = (chunks + chunk) * shard_rows
            rel_query_ref[reversed_rows, lanes] = table_ref[source, at : at + shard_rows, :]

    places = sources * QROWS
    held = rows_dev * chunks
    request_id = lax.broadcasted_iota(jnp.int32, (requests, places), 0)
    place = lax.broadcasted_iota(jnp.int32, (requests, places), 1)
    place_request = shard_of(place // QROWS) * rows_dev + (place % QROWS) // chunks
    used = (place % QROWS < held) & (place_request == request_id)
    slots = jnp.broadcast_to(slot_of_ref[...].astype(jnp.float32), (QROWS, requests))
    slot_at = dot_f32(slots.astype(jnp.bfloat16), jnp.where(used, 1.0, 0.0).astype(jnp.bfloat16))
    wanted = lax.broadcasted_iota(jnp.int32, (QROWS, places), 0)
    place = lax.broadcasted_iota(jnp.int32, (QROWS, places), 1) % QROWS
    wanted_slot = first_slot + sum(
        jnp.where(wanted // chunks == place_held, order[place_held], 0)
        for place_held in range(rows_dev)
    )
    hit = (
        (slot_at == wanted_slot.astype(jnp.float32))
        & (place % chunks == wanted % chunks)
        & (place < held)
        & (wanted < held)
    )
    query_rows = jnp.concatenate(
        [queries_ref[source, query_at:, :].astype(jnp.float32) for source in range(sources)], axis=0
    )
    own_queries = dot_f32(
        jnp.where(hit, 1.0, 0.0).astype(jnp.bfloat16), query_rows.astype(jnp.bfloat16)
    )

    pair_id = lax.broadcasted_iota(jnp.int32, (pairs, cols), 0)
    head_id = lax.broadcasted_iota(jnp.int32, (pairs, cols), 1) // HD
    query_heads = jnp.zeros((pairs, cols), jnp.float32)
    query_columns = []
    for index in range(rows_dev):
        own = own_queries[index * chunks : (index + 1) * chunks]
        query = jnp.concatenate([own[chunk : chunk + 1] for chunk in range(chunks)], axis=1)
        query_heads = jnp.where(pair_id == index * heads + head_id, query, query_heads)
        query_columns.append(
            jnp.concatenate(
                [
                    jnp.broadcast_to(own[chunk : chunk + 1], (LANES, LANES)).T
                    for chunk in range(chunks)
                ],
                axis=0,
            )
        )
    by_bucket = lax.dot_general(
        query_heads.astype(jnp.bfloat16), rel_key_ref[...], NT, preferred_element_type=jnp.float32
    )
    shifted = jnp.concatenate((by_bucket[:, 1:], by_bucket[:, :1]), axis=1)
    rel_query = rel_query_ref[...].astype(jnp.float32).T.astype(jnp.bfloat16)
    left = jnp.concatenate((rel_query,) + split3(shifted), axis=0)

    pair_row = lax.broadcasted_iota(jnp.int32, (pairs, 1), 0)
    pair_length = jnp.full((pairs, 1), lengths[0], jnp.float32)
    for index in range(1, rows_dev):
        pair_length = jnp.where(pair_row >= index * heads, lengths[index], pair_length)
    table_id = lax.broadcasted_iota(jnp.int32, (BUCKETS, BLOCK), 0)
    table_half = (table_id - BUCKETS // 2).astype(jnp.bfloat16)

    def block_scores(index, offset):
        here = slice(offset, offset + BLOCK)
        bucket = bucket_ref[pl.ds(order[index], 1), here]
        row = (jnp.maximum(bucket - 1, 0) - BUCKETS // 2).astype(jnp.bfloat16)
        one_hot = jnp.where(table_half == row, jnp.bfloat16(1.0), jnp.bfloat16(0.0))
        found = dot_f32(left, one_hot)
        keys = key_ref[index, here, :] if index else first_key_ref[here, :]
        query_column = jnp.concatenate([query_columns[index]] * (BLOCK // LANES), axis=1)
        products = keys.astype(jnp.float32).T * (found[:cols] + query_column)
        along = found[cols : cols + pairs] + (
            found[cols + pairs : cols + 2 * pairs] + found[cols + 2 * pairs :]
        )
        along = jnp.where(bucket == 0, by_bucket[:, 0:1], along)
        sums = [
            jnp.sum(products[head * HD : (head + 1) * HD], axis=0, keepdims=True)
            for head in range(heads)
        ]
        own_pairs = slice(index * heads, (index + 1) * heads)
        score_ref[own_pairs, here] = jnp.concatenate(sums, axis=0) + along[own_pairs]

    def attend(sizes):
        width = max(sizes)
        for index in range(rows_dev):
            own_pairs = slice(index * heads, (index + 1) * heads)
            if sizes[index] < width:
                score_ref[own_pairs, sizes[index] : width] = jnp.zeros(
                    (heads, width - sizes[index]), jnp.float32
                )
            for offset in range(0, sizes[index], BLOCK):
                if index and offset % REGION == 0:
                    load_keys(index, offset // REGION).wait()
                block_scores(index, offset)
        place = lax.broadcasted_iota(jnp.int32, (pairs, width), 1)
        live = place.astype(jnp.float32) < pair_length
        scores = score_ref[:, 0:width] * (1.0 / math.sqrt(3.0 * HD))
        scores = jnp.where(live, scores, masked_score)
        highest = jnp.max(scores, axis=1, keepdims=True)
        exponent = jnp.where(live, jnp.exp(scores - highest), 0.0)
        weights = (exponent / jnp.sum(exponent, axis=1, keepdims=True)).astype(jnp.bfloat16)
        contexts = [jnp.zeros((1, cols), jnp.float32)] * rows_dev
        for index in range(rows_dev):
            size = sizes[index]
            for part in range(size // REGION):
                load_values(index, part).wait()
            spread = dot_f32(weights[:, 0:size], value_ref[index, 0:size, :])
            spread = jnp.where(pair_id == index * heads + head_id, spread, 0.0)
            context = jnp.sum(spread, axis=0, keepdims=True)
            contexts = [
                jnp.where(order[index] == row, context, other)
                for row, other in enumerate(contexts)
            ]
        context = jnp.concatenate(contexts, axis=0).astype(jnp.bfloat16)
        out_ref[...] = jnp.broadcast_to(context[None], out_ref.shape)

    steps = range(REGION, MAXLEN + 1, REGION)
    for sizes in itertools.product((REGION, MAXLEN), *[steps] * (rows_dev - 1)):
        if max(sizes) > sizes[0]:
            continue
        taken = (lengths[0] > REGION) == (sizes[0] > REGION)
        for index in range(1, rows_dev):
            taken &= lengths[index] > sizes[index] - REGION
            taken &= lengths[index] <= sizes[index]
        pl.when(taken)(functools.partial(attend, sizes))


def finish_kernel(tp_size, slot_of_ref, contexts_ref, tokens_ref, gain_ref, bias_ref, *refs):
    w_refs, (out_ref, norm_ref) = refs[:tp_size], refs[tp_size:]
    rows_dev, width = tokens_ref.shape
    cols = out_ref.shape[1]
    requests = slot_of_ref.shape[1]
    first_row = lax.axis_index("req") * rows_dev
    tp_index = lax.axis_index("tp")
    lane = lax.broadcasted_iota(jnp.int32, (8, requests), 1)
    row = lax.broadcasted_iota(jnp.int32, (8, requests), 0)
    slots = jnp.broadcast_to(slot_of_ref[...].astype(jnp.float32), (8, requests))
    slot = jnp.sum(jnp.where(lane == first_row + row, slots, 0.0), axis=1, keepdims=True)
    chosen = jnp.where(lane.astype(jnp.float32) == slot, 1.0, 0.0).astype(jnp.bfloat16)
    products = []
    gathered = jnp.concatenate(
        [
            jnp.concatenate(
                [
                    contexts_ref[source * tp_size + (tp_index ^ step)].astype(jnp.float32)
                    for source in range(requests // rows_dev)
                ],
                axis=0,
            )
            for step in range(tp_size)
        ],
        axis=1,
    )
    context = dot_f32(chosen, gathered.astype(jnp.bfloat16)).astype(jnp.bfloat16)
    for step in range(tp_size):
        products.append(dot_f32(context[:, step * cols : (step + 1) * cols], w_refs[step][...]))
    while len(products) > 1:
        products = [a + b for a, b in zip(products[::2], products[1::2], strict=True)]
    product = products[0]
    attended = product[0:rows_dev] + tokens_ref[...].astype(jnp.float32)
    mean = jnp.mean(attended, axis=1, keepdims=True)
    centred = attended - mean
    variance = jnp.mean(centred * centred, axis=1, keepdims=True)
    norm_ref[...] = centred * lax.rsqrt(variance + epsilon)
    own_cols = norm_ref[:, pl.ds(pl.multiple_of(tp_index * cols, cols), cols)]
    out_ref[...] = (own_cols * gain_ref[...] + bias_ref[...]).astype(out_ref.dtype)


def xor_permute(block, tp_size, bit):
    return lax.ppermute(block, "tp", [(i, i ^ bit) for i in range(tp_size)])


def gather_half(block, tp_size):
    return {0: block, 2: xor_permute(block, tp_size, 2), 1: xor_permute(block, tp_size, 1)}


def complete(held, tp_size):
    return [held[0], held[1], held[2], xor_permute(held[2], tp_size, 1)]


def make_per_device(req_size, tp_size):
    def per_device(
        tokens,
        slot_of,
        key_cache,
        value_cache,
        cache_len,
        rel_bucket,
        rel_table,
        w_query,
        w_key,
        w_out,
        out_gain,
        out_bias,
    ):
        rows_dev, width = tokens.shape
        slots = slot_of.reshape(1, -1)
        cols = w_query.shape[1]
        chunks = cols // LANES
        shard_rows = rel_table.shape[0]
        pitch = -(-shard_rows // 8) * 8
        table_rows = 2 * chunks * pitch
        block_rows = table_rows + QROWS
        block = pl.pallas_call(
            project_kernel,
            out_shape=jax.ShapeDtypeStruct((block_rows, LANES), jnp.bfloat16),
            in_specs=[ANY] * 4,
            out_specs=VMEM,
            scratch_shapes=[
                pltpu.VMEM(tokens.shape, jnp.bfloat16),
                pltpu.VMEM(rel_table.shape, jnp.bfloat16),
                pltpu.VMEM(w_query.shape, jnp.bfloat16),
                pltpu.VMEM(w_key.shape, jnp.bfloat16),
                pltpu.SemaphoreType.DMA((4,)),
            ],
            name="project",
            compiler_params=ROOM,
        )(*[in_hbm(array) for array in (tokens, rel_table, w_query, w_key)])
        half = req_size // 2
        mirror = lax.ppermute(block, "req", [(i, (i + half) % req_size) for i in range(req_size)])
        send = pl.pallas_call(
            spread_kernel,
            out_shape=jax.ShapeDtypeStruct((half, 2 * block_rows, LANES), jnp.bfloat16),
            in_specs=[VMEM] * 2,
            out_specs=VMEM,
            name="spread",
            compiler_params=ROOM,
        )(block, mirror)
        halves = [list(range(half)), list(range(half, req_size))]
        received = lax.all_to_all(send, "req", 0, 0, axis_index_groups=halves)
        w_blocks = gather_half(lax.optimization_barrier((block, w_out))[1], tp_size)
        received = received.reshape(req_size, block_rows, LANES)
        by_halves = shard_rows % 16 == 0
        if by_halves:
            table = received
        else:
            received = received.reshape(half, 2, block_rows, LANES).transpose(1, 0, 2, 3)
            first = lax.axis_index("req") < half
            received = jnp.where(first, received, received[::-1])
            received = received.reshape(req_size, block_rows, LANES)
            table = received[:, :table_rows].reshape(req_size, 2, chunks, pitch, LANES)
            table = table[:, :, :, :shard_rows]
            table = jnp.stack((table[:, 0], table[::-1, 1]), axis=0)
            table = table.transpose(0, 2, 1, 3, 4).reshape(1, -1, LANES)
        lengths = cache_len.reshape(1, rows_dev)
        first_key = pl.pallas_call(
            keep_kernel,
            out_shape=pltpu.VMEM(key_cache.shape[1:], key_cache.dtype),
            in_specs=[VMEM, ANY],
            out_specs=VMEM,
            scratch_shapes=[pltpu.SemaphoreType.DMA],
            name="keep",
            compiler_params=ROOM,
        )(lengths, in_hbm(key_cache))
        contexts = pl.pallas_call(
            functools.partial(attend_kernel, by_halves),
            out_shape=jax.ShapeDtypeStruct((req_size * tp_size, rows_dev, cols), jnp.bfloat16),
            in_specs=[VMEM] * 6 + [ANY, ANY],
            out_specs=VMEM,
            scratch_shapes=[
                pltpu.VMEM(key_cache.shape, jnp.bfloat16),
                pltpu.VMEM(value_cache.shape, jnp.bfloat16),
                pltpu.VMEM((BUCKETS, cols), jnp.bfloat16),
                pltpu.VMEM((BUCKETS, cols), jnp.bfloat16),
                pltpu.VMEM((rows_dev * cols // HD, MAXLEN), jnp.float32),
                pltpu.SemaphoreType.DMA((rows_dev, MAXLEN // REGION)),
                pltpu.SemaphoreType.DMA((rows_dev, MAXLEN // REGION)),
            ],
            name="attend",
            compiler_params=ROOM,
        )(
            slots,
            lengths,
            table,
            received,
            rel_bucket,
            first_key,
            in_hbm(key_cache),
            in_hbm(value_cache),
        )
        contexts, w_blocks = lax.optimization_barrier((contexts, complete(w_blocks, tp_size)))
        contexts = lax.all_to_all(contexts, ("req", "tp"), 0, 0)
        return pl.pallas_call(
            functools.partial(finish_kernel, tp_size),
            out_shape=jax.ShapeDtypeStruct((rows_dev, cols), jnp.bfloat16),
            in_specs=[VMEM] * (5 + tp_size),
            out_specs=VMEM,
            scratch_shapes=[pltpu.VMEM((rows_dev, width), jnp.float32)],
            name="finish",
            compiler_params=ROOM,
        )(
            slots,
            contexts,
            tokens,
            out_gain.reshape(1, cols),
            out_bias.reshape(1, cols),
            *[in_vmem(block) for block in w_blocks],
        )

    return per_device


def solution(mesh):
    in_specs = (
        P("req", None),
        P(),
        P("req", None, "tp"),
        P("req", None, "tp"),
        P("req"),
        P("req", None),
        P("req", None),
        P(None, "tp"),
        P(None, "tp"),
        P("tp", None),
        P("tp"),
        P("tp"),
    )
    return jax.shard_map(
        make_per_device(mesh.shape["req"], mesh.shape["tp"]),
        mesh=mesh,
        in_specs=in_specs,
        out_specs=P("req", "tp"),
        check_vma=False,
    )
```

```python
import functools
import itertools
import math

import jax
import jax.numpy as jnp
from jax import lax
from jax.experimental import pallas as pl
from jax.experimental.pallas import tpu as pltpu
from jax.sharding import PartitionSpec as P

HD = 64
BUCKETS = 512
MAXLEN = 1536
BLOCK = 256
REGION = 512
LANES = 128
QROWS = 8

epsilon = 1e-06
masked_score = -1e30

VMEM = pl.BlockSpec(memory_space=pltpu.VMEM)
SMEM = pl.BlockSpec(memory_space=pltpu.SMEM)
ANY = pl.BlockSpec(memory_space=pl.ANY)
ROOM = pltpu.CompilerParams(vmem_limit_bytes=24 * 2**20)
NT = (((1,), (1,)), ((), ()))


def dot_f32(a, b):
    return jnp.dot(a, b, preferred_element_type=jnp.float32)


def in_hbm(array):
    return pltpu.with_memory_space_constraint(array, pltpu.HBM)


def in_vmem(array):
    return pltpu.with_memory_space_constraint(array, pltpu.VMEM)


def project_kernel(
    tokens_hbm, table_hbm, w_query_hbm, w_key_hbm, out_ref,
    tokens_ref, table_ref, w_query_ref, w_key_ref, sems,
):
    loads = [
        pltpu.make_async_copy(source, target, sems.at[index])
        for index, (source, target) in enumerate(
            (
                (table_hbm, table_ref),
                (tokens_hbm, tokens_ref),
                (w_query_hbm, w_query_ref),
                (w_key_hbm, w_key_ref),
            )
        )
    ]
    for load in loads:
        load.start()
    rows, rows_dev = table_ref.shape[0], tokens_ref.shape[0]
    cols = w_query_ref.shape[1]
    chunks = cols // LANES
    query_at = out_ref.shape[0] - QROWS
    pitch = query_at // (2 * chunks)
    row_id = lax.broadcasted_iota(jnp.int32, (rows, rows), 0)
    column_id = lax.broadcasted_iota(jnp.int32, (rows, rows), 1)
    flip = jnp.where(row_id + column_id == rows - 1, 1.0, 0.0).astype(jnp.bfloat16)
    loads[0].wait()
    table = table_ref[...].astype(jnp.float32)
    centred = table - jnp.mean(table, axis=1, keepdims=True)
    variance = jnp.mean(centred * centred, axis=1, keepdims=True)
    normed = (centred * lax.rsqrt(variance + epsilon)).astype(jnp.bfloat16)
    loads[1].wait()
    loads[2].wait()
    rel_query = dot_f32(normed, w_query_ref[...]).astype(jnp.bfloat16)
    rel_query = dot_f32(flip, rel_query).astype(jnp.bfloat16)
    queries = dot_f32(tokens_ref[...], w_query_ref[...])
    query_rows = [
        queries[row : row + 1, chunk * LANES : (chunk + 1) * LANES]
        for row in range(rows_dev)
        for chunk in range(chunks)
    ]
    query_rows.append(jnp.zeros((QROWS - len(query_rows), LANES), jnp.float32))
    query_block = jnp.concatenate(query_rows, axis=0).astype(jnp.bfloat16)
    for chunk in range(chunks):
        at = (chunks + chunk) * pitch
        out_ref[at : at + rows, :] = rel_query[:, chunk * LANES : (chunk + 1) * LANES]
    out_ref[query_at:, :] = query_block
    loads[3].wait()
    rel_key = dot_f32(normed, w_key_ref[...]).astype(jnp.bfloat16)
    for chunk in range(chunks):
        at = chunk * pitch
        out_ref[at : at + rows, :] = rel_key[:, chunk * LANES : (chunk + 1) * LANES]


def longest_first(cache_len_ref):
    rows_dev = cache_len_ref.shape[1]
    lane = lax.broadcasted_iota(jnp.int32, (1, rows_dev), 1)
    cache_len = cache_len_ref[...].astype(jnp.float32)
    lengths = [jnp.sum(jnp.where(lane == slot, cache_len, 0.0)) for slot in range(rows_dev)]
    longest, first = lengths[0], jnp.int32(0)
    for slot in range(1, rows_dev):
        first = jnp.where(lengths[slot] > longest, slot, first)
        longest = jnp.maximum(lengths[slot], longest)
    order, ordered = [first], [longest]
    for place in range(1, rows_dev):
        order.append(jnp.where(first < place, place, place - 1))
        ordered.append(jnp.where(first < place, lengths[place], lengths[place - 1]))
    return order, ordered


def keep_kernel(cache_len_ref, key_hbm, out_ref, sem):
    order, _ = longest_first(cache_len_ref)
    load = pltpu.make_async_copy(key_hbm.at[order[0]], out_ref, sem)
    load.start()
    load.wait()


def spread_kernel(own_ref, mirror_ref, out_hbm, sems):
    rows = own_ref.shape[0]
    for part, block_ref in enumerate((own_ref, mirror_ref)):
        for peer in range(out_hbm.shape[0]):
            place = out_hbm.at[peer, pl.ds(part * rows, rows)]
            pltpu.make_async_copy(block_ref, place, sems.at[part]).start()
    for part in range(2):
        filled = out_hbm.at[:, pl.ds(part * rows, rows)]
        pltpu.make_async_copy(filled, filled, sems.at[part]).wait()


def split3(value):
    high = value.astype(jnp.bfloat16)
    rest = value - high.astype(jnp.float32)
    middle = rest.astype(jnp.bfloat16)
    low = (rest - middle.astype(jnp.float32)).astype(jnp.bfloat16)
    return high, middle, low


def attend_kernel(
    by_halves, slot_of_ref, cache_len_ref, table_ref, queries_ref, bucket_ref, first_key_ref, key_hbm, value_hbm,
    out_ref, key_ref, value_ref, rel_key_ref, rel_query_ref, score_ref, key_sems, value_sems,
):
    rows_dev, cols = key_ref.shape[0], key_ref.shape[2]
    heads = cols // HD
    pairs = rows_dev * heads
    chunks = cols // LANES
    shards, shard_rows = table_ref.shape[0], BUCKETS // table_ref.shape[0]
    requests = slot_of_ref.shape[1]
    query_at = queries_ref.shape[1] - QROWS
    first_slot = lax.axis_index("req") * rows_dev

    order, lengths = longest_first(cache_len_ref)

    def load(source, target, sems, place, part):
        rows = pl.ds(part * REGION, REGION)
        return pltpu.make_async_copy(
            source.at[order[place], rows], target.at[place, rows], sems.at[place, part]
        )

    load_keys = functools.partial(load, key_hbm, key_ref, key_sems)
    load_values = functools.partial(load, value_hbm, value_ref, value_sems)
    parts = MAXLEN // REGION

    def start_loads(place, part):
        if place:
            load_keys(place, part).start()
        load_values(place, part).start()

    for place in reversed(range(rows_dev)):
        start_loads(place, 0)

    @pl.when(lengths[0] > REGION)
    def _():
        for part in range(1, parts):
            start_loads(0, part)

    for place in range(1, rows_dev):
        for part in range(1, parts):

            @pl.when(lengths[place] > part * REGION)
            def _():
                start_loads(place, part)

    sources = queries_ref.shape[0]
    own_half = lax.axis_index("req") // (sources // 2)

    def shard_of(source):
        if not by_halves:
            return source
        return (own_half ^ (source % 2)) * (sources // 2) + source // 2

    for source in range(shards):
        shard = shard_of(source)
        rows = pl.ds(shard * shard_rows, shard_rows)
        reversed_rows = pl.ds((shards - 1 - shard) * shard_rows, shard_rows)
        if by_halves:
            rows = pl.ds(pl.multiple_of(rows.start, shard_rows), shard_rows)
            reversed_rows = pl.ds(pl.multiple_of(reversed_rows.start, shard_rows), shard_rows)
        for chunk in range(chunks):
            lanes = slice(chunk * LANES, (chunk + 1) * LANES)
            at = chunk * shard_rows
            rel_key_ref[rows, lanes] = table_ref[source, at : at + shard_rows, :]
            at = (chunks + chunk) * shard_rows
            rel_query_ref[reversed_rows, lanes] = table_ref[source, at : at + shard_rows, :]

    places = sources * QROWS
    held = rows_dev * chunks
    request_id = lax.broadcasted_iota(jnp.int32, (requests, places), 0)
    place = lax.broadcasted_iota(jnp.int32, (requests, places), 1)
    place_request = shard_of(place // QROWS) * rows_dev + (place % QROWS) // chunks
    used = (place % QROWS < held) & (place_request == request_id)
    slots = jnp.broadcast_to(slot_of_ref[...].astype(jnp.float32), (QROWS, requests))
    slot_at = dot_f32(slots.astype(jnp.bfloat16), jnp.where(used, 1.0, 0.0).astype(jnp.bfloat16))
    wanted = lax.broadcasted_iota(jnp.int32, (QROWS, places), 0)
    place = lax.broadcasted_iota(jnp.int32, (QROWS, places), 1) % QROWS
    wanted_slot = first_slot + sum(
        jnp.where(wanted // chunks == place_held, order[place_held], 0)
        for place_held in range(rows_dev)
    )
    hit = (
        (slot_at == wanted_slot.astype(jnp.float32))
        & (place % chunks == wanted % chunks)
        & (place < held)
        & (wanted < held)
    )
    query_rows = jnp.concatenate(
        [queries_ref[source, query_at:, :].astype(jnp.float32) for source in range(sources)], axis=0
    )
    own_queries = dot_f32(
        jnp.where(hit, 1.0, 0.0).astype(jnp.bfloat16), query_rows.astype(jnp.bfloat16)
    )

    pair_id = lax.broadcasted_iota(jnp.int32, (pairs, cols), 0)
    head_id = lax.broadcasted_iota(jnp.int32, (pairs, cols), 1) // HD
    query_heads = jnp.zeros((pairs, cols), jnp.float32)
    query_columns = []
    for index in range(rows_dev):
        own = own_queries[index * chunks : (index + 1) * chunks]
        query = jnp.concatenate([own[chunk : chunk + 1] for chunk in range(chunks)], axis=1)
        query_heads = jnp.where(pair_id == index * heads + head_id, query, query_heads)
        query_columns.append(
            jnp.concatenate(
                [
                    jnp.broadcast_to(own[chunk : chunk + 1], (LANES, LANES)).T
                    for chunk in range(chunks)
                ],
                axis=0,
            )
        )
    by_bucket = lax.dot_general(
        query_heads.astype(jnp.bfloat16), rel_key_ref[...], NT, preferred_element_type=jnp.float32
    )
    shifted = jnp.concatenate((by_bucket[:, 1:], by_bucket[:, :1]), axis=1)
    rel_query = rel_query_ref[...].astype(jnp.float32).T.astype(jnp.bfloat16)
    left = jnp.concatenate((rel_query,) + split3(shifted), axis=0)

    pair_row = lax.broadcasted_iota(jnp.int32, (pairs, 1), 0)
    pair_length = jnp.full((pairs, 1), lengths[0], jnp.float32)
    for index in range(1, rows_dev):
        pair_length = jnp.where(pair_row >= index * heads, lengths[index], pair_length)
    table_id = lax.broadcasted_iota(jnp.int32, (BUCKETS, BLOCK), 0)
    table_half = (table_id - BUCKETS // 2).astype(jnp.bfloat16)

    def block_scores(index, offset):
        here = slice(offset, offset + BLOCK)
        bucket = bucket_ref[pl.ds(order[index], 1), here]
        row = (jnp.maximum(bucket - 1, 0) - BUCKETS // 2).astype(jnp.bfloat16)
        one_hot = jnp.where(table_half == row, jnp.bfloat16(1.0), jnp.bfloat16(0.0))
        found = dot_f32(left, one_hot)
        keys = key_ref[index, here, :] if index else first_key_ref[here, :]
        query_column = jnp.concatenate([query_columns[index]] * (BLOCK // LANES), axis=1)
        products = keys.astype(jnp.float32).T * (found[:cols] + query_column)
        along = found[cols : cols + pairs] + (
            found[cols + pairs : cols + 2 * pairs] + found[cols + 2 * pairs :]
        )
        along = jnp.where(bucket == 0, by_bucket[:, 0:1], along)
        sums = [
            jnp.sum(products[head * HD : (head + 1) * HD], axis=0, keepdims=True)
            for head in range(heads)
        ]
        own_pairs = slice(index * heads, (index + 1) * heads)
        score_ref[own_pairs, here] = jnp.concatenate(sums, axis=0) + along[own_pairs]

    def attend(sizes):
        width = max(sizes)
        for index in range(rows_dev):
            own_pairs = slice(index * heads, (index + 1) * heads)
            if sizes[index] < width:
                score_ref[own_pairs, sizes[index] : width] = jnp.zeros(
                    (heads, width - sizes[index]), jnp.float32
                )
            for offset in range(0, sizes[index], BLOCK):
                if index and offset % REGION == 0:
                    load_keys(index, offset // REGION).wait()
                block_scores(index, offset)
        place = lax.broadcasted_iota(jnp.int32, (pairs, width), 1)
        live = place.astype(jnp.float32) < pair_length
        scores = score_ref[:, 0:width] * (1.0 / math.sqrt(3.0 * HD))
        scores = jnp.where(live, scores, masked_score)
        highest = jnp.max(scores, axis=1, keepdims=True)
        exponent = jnp.where(live, jnp.exp(scores - highest), 0.0)
        weights = (exponent / jnp.sum(exponent, axis=1, keepdims=True)).astype(jnp.bfloat16)
        contexts = [jnp.zeros((1, cols), jnp.float32)] * rows_dev
        for index in range(rows_dev):
            size = sizes[index]
            for part in range(size // REGION):
                load_values(index, part).wait()
            spread = dot_f32(weights[:, 0:size], value_ref[index, 0:size, :])
            spread = jnp.where(pair_id == index * heads + head_id, spread, 0.0)
            context = jnp.sum(spread, axis=0, keepdims=True)
            contexts = [
                jnp.where(order[index] == row, context, other)
                for row, other in enumerate(contexts)
            ]
        context = jnp.concatenate(contexts, axis=0).astype(jnp.bfloat16)
        out_ref[...] = jnp.broadcast_to(context[None], out_ref.shape)

    steps = range(REGION, MAXLEN + 1, REGION)
    for sizes in itertools.product((REGION, MAXLEN), *[steps] * (rows_dev - 1)):
        if max(sizes) > sizes[0]:
            continue
        taken = (lengths[0] > REGION) == (sizes[0] > REGION)
        for index in range(1, rows_dev):
            taken &= lengths[index] > sizes[index] - REGION
            taken &= lengths[index] <= sizes[index]
        pl.when(taken)(functools.partial(attend, sizes))


def finish_kernel(tp_size, slot_of_ref, contexts_ref, tokens_ref, gain_ref, bias_ref, *refs):
    w_refs, (out_ref, norm_ref) = refs[:tp_size], refs[tp_size:]
    rows_dev, width = tokens_ref.shape
    cols = out_ref.shape[1]
    requests = slot_of_ref.shape[1]
    first_row = lax.axis_index("req") * rows_dev
    tp_index = lax.axis_index("tp")
    lane = lax.broadcasted_iota(jnp.int32, (8, requests), 1)
    row = lax.broadcasted_iota(jnp.int32, (8, requests), 0)
    slots = jnp.broadcast_to(slot_of_ref[...].astype(jnp.float32), (8, requests))
    slot = jnp.sum(jnp.where(lane == first_row + row, slots, 0.0), axis=1, keepdims=True)
    chosen = jnp.where(lane.astype(jnp.float32) == slot, 1.0, 0.0).astype(jnp.bfloat16)
    products = []
    gathered = jnp.concatenate(
        [
            jnp.concatenate(
                [
                    contexts_ref[source * tp_size + (tp_index ^ step)].astype(jnp.float32)
                    for source in range(requests // rows_dev)
                ],
                axis=0,
            )
            for step in range(tp_size)
        ],
        axis=1,
    )
    context = dot_f32(chosen, gathered.astype(jnp.bfloat16)).astype(jnp.bfloat16)
    for step in range(tp_size):
        products.append(dot_f32(context[:, step * cols : (step + 1) * cols], w_refs[step][...]))
    while len(products) > 1:
        products = [a + b for a, b in zip(products[::2], products[1::2], strict=True)]
    product = products[0]
    attended = product[0:rows_dev] + tokens_ref[...].astype(jnp.float32)
    mean = jnp.mean(attended, axis=1, keepdims=True)
    centred = attended - mean
    variance = jnp.mean(centred * centred, axis=1, keepdims=True)
    norm_ref[...] = centred * lax.rsqrt(variance + epsilon)
    own_cols = norm_ref[:, pl.ds(pl.multiple_of(tp_index * cols, cols), cols)]
    out_ref[...] = (own_cols * gain_ref[...] + bias_ref[...]).astype(out_ref.dtype)


def xor_permute(block, tp_size, bit):
    return lax.ppermute(block, "tp", [(i, i ^ bit) for i in range(tp_size)])


def gather_half(block, tp_size):
    return {0: block, 2: xor_permute(block, tp_size, 2), 1: xor_permute(block, tp_size, 1)}


def complete(held, tp_size):
    return [held[0], held[1], held[2], xor_permute(held[2], tp_size, 1)]


def make_per_device(req_size, tp_size):
    def per_device(
        tokens,
        slot_of,
        key_cache,
        value_cache,
        cache_len,
        rel_bucket,
        rel_table,
        w_query,
        w_key,
        w_out,
        out_gain,
        out_bias,
    ):
        rows_dev, width = tokens.shape
        slots = slot_of.reshape(1, -1)
        cols = w_query.shape[1]
        chunks = cols // LANES
        shard_rows = rel_table.shape[0]
        pitch = -(-shard_rows // 8) * 8
        table_rows = 2 * chunks * pitch
        block_rows = table_rows + QROWS
        block = pl.pallas_call(
            project_kernel,
            out_shape=jax.ShapeDtypeStruct((block_rows, LANES), jnp.bfloat16),
            in_specs=[ANY] * 4,
            out_specs=VMEM,
            scratch_shapes=[
                pltpu.VMEM(tokens.shape, jnp.bfloat16),
                pltpu.VMEM(rel_table.shape, jnp.bfloat16),
                pltpu.VMEM(w_query.shape, jnp.bfloat16),
                pltpu.VMEM(w_key.shape, jnp.bfloat16),
                pltpu.SemaphoreType.DMA((4,)),
            ],
            name="project",
            compiler_params=ROOM,
        )(*[in_hbm(array) for array in (tokens, rel_table, w_query, w_key)])
        half = req_size // 2
        mirror = lax.ppermute(block, "req", [(i, (i + half) % req_size) for i in range(req_size)])
        send = pl.pallas_call(
            spread_kernel,
            out_shape=jax.ShapeDtypeStruct((half, 2 * block_rows, LANES), jnp.bfloat16),
            in_specs=[VMEM] * 2,
            out_specs=ANY,
            scratch_shapes=[pltpu.SemaphoreType.DMA((2,))],
            name="spread",
            compiler_params=ROOM,
        )(block, mirror)
        halves = [list(range(half)), list(range(half, req_size))]
        received = lax.all_to_all(send, "req", 0, 0, axis_index_groups=halves)
        w_blocks = gather_half(lax.optimization_barrier((block, w_out))[1], tp_size)
        received = received.reshape(req_size, block_rows, LANES)
        by_halves = shard_rows % 16 == 0
        if by_halves:
            table = received
        else:
            received = received.reshape(half, 2, block_rows, LANES).transpose(1, 0, 2, 3)
            first = lax.axis_index("req") < half
            received = jnp.where(first, received, received[::-1])
            received = received.reshape(req_size, block_rows, LANES)
            table = received[:, :table_rows].reshape(req_size, 2, chunks, pitch, LANES)
            table = table[:, :, :, :shard_rows]
            table = jnp.stack((table[:, 0], table[::-1, 1]), axis=0)
            table = table.transpose(0, 2, 1, 3, 4).reshape(1, -1, LANES)
        lengths = cache_len.reshape(1, rows_dev)
        first_key = pl.pallas_call(
            keep_kernel,
            out_shape=pltpu.VMEM(key_cache.shape[1:], key_cache.dtype),
            in_specs=[VMEM, ANY],
            out_specs=VMEM,
            scratch_shapes=[pltpu.SemaphoreType.DMA],
            name="keep",
            compiler_params=ROOM,
        )(lengths, in_hbm(key_cache))
        contexts = pl.pallas_call(
            functools.partial(attend_kernel, by_halves),
            out_shape=jax.ShapeDtypeStruct((req_size * tp_size, rows_dev, cols), jnp.bfloat16),
            in_specs=[VMEM] * 6 + [ANY, ANY],
            out_specs=VMEM,
            scratch_shapes=[
                pltpu.VMEM(key_cache.shape, jnp.bfloat16),
                pltpu.VMEM(value_cache.shape, jnp.bfloat16),
                pltpu.VMEM((BUCKETS, cols), jnp.bfloat16),
                pltpu.VMEM((BUCKETS, cols), jnp.bfloat16),
                pltpu.VMEM((rows_dev * cols // HD, MAXLEN), jnp.float32),
                pltpu.SemaphoreType.DMA((rows_dev, MAXLEN // REGION)),
                pltpu.SemaphoreType.DMA((rows_dev, MAXLEN // REGION)),
            ],
            name="attend",
            compiler_params=ROOM,
        )(
            slots,
            lengths,
            table,
            received,
            rel_bucket,
            first_key,
            in_hbm(key_cache),
            in_hbm(value_cache),
        )
        contexts, w_blocks = lax.optimization_barrier((contexts, complete(w_blocks, tp_size)))
        contexts = lax.all_to_all(contexts, ("req", "tp"), 0, 0)
        return pl.pallas_call(
            functools.partial(finish_kernel, tp_size),
            out_shape=jax.ShapeDtypeStruct((rows_dev, cols), jnp.bfloat16),
            in_specs=[VMEM] * (5 + tp_size),
            out_specs=VMEM,
            scratch_shapes=[pltpu.VMEM((rows_dev, width), jnp.float32)],
            name="finish",
            compiler_params=ROOM,
        )(
            slots,
            contexts,
            tokens,
            out_gain.reshape(1, cols),
            out_bias.reshape(1, cols),
            *[in_vmem(block) for block in w_blocks],
        )

    return per_device


def solution(mesh):
    in_specs = (
        P("req", None),
        P(),
        P("req", None, "tp"),
        P("req", None, "tp"),
        P("req"),
        P("req", None),
        P("req", None),
        P(None, "tp"),
        P(None, "tp"),
        P("tp", None),
        P("tp"),
        P("tp"),
    )
    return jax.shard_map(
        make_per_device(mesh.shape["req"], mesh.shape["tp"]),
        mesh=mesh,
        in_specs=in_specs,
        out_specs=P("req", "tp"),
        check_vma=False,
    )
```

```python
import functools
import itertools
import math

import jax
import jax.numpy as jnp
from jax import lax
from jax.experimental import pallas as pl
from jax.experimental.pallas import tpu as pltpu
from jax.sharding import PartitionSpec as P

HD = 64
BUCKETS = 512
MAXLEN = 1536
BLOCK = 256
REGION = 512
LANES = 128
QROWS = 8

epsilon = 1e-06
masked_score = -1e30

VMEM = pl.BlockSpec(memory_space=pltpu.VMEM)
SMEM = pl.BlockSpec(memory_space=pltpu.SMEM)
ANY = pl.BlockSpec(memory_space=pl.ANY)
ROOM = pltpu.CompilerParams(vmem_limit_bytes=24 * 2**20)
NT = (((1,), (1,)), ((), ()))


def dot_f32(a, b):
    return jnp.dot(a, b, preferred_element_type=jnp.float32)


def in_hbm(array):
    return pltpu.with_memory_space_constraint(array, pltpu.HBM)


def in_vmem(array):
    return pltpu.with_memory_space_constraint(array, pltpu.VMEM)


def project_kernel(
    tokens_hbm, table_hbm, w_query_hbm, w_key_hbm, out_ref,
    tokens_ref, table_ref, w_query_ref, w_key_ref, sems,
):
    loads = [
        pltpu.make_async_copy(source, target, sems.at[index])
        for index, (source, target) in enumerate(
            (
                (table_hbm, table_ref),
                (tokens_hbm, tokens_ref),
                (w_query_hbm, w_query_ref),
                (w_key_hbm, w_key_ref),
            )
        )
    ]
    for load in loads:
        load.start()
    rows, rows_dev = table_ref.shape[0], tokens_ref.shape[0]
    cols = w_query_ref.shape[1]
    chunks = cols // LANES
    query_at = out_ref.shape[0] - QROWS
    pitch = query_at // (2 * chunks)
    row_id = lax.broadcasted_iota(jnp.int32, (rows, rows), 0)
    column_id = lax.broadcasted_iota(jnp.int32, (rows, rows), 1)
    flip = jnp.where(row_id + column_id == rows - 1, 1.0, 0.0).astype(jnp.bfloat16)
    loads[0].wait()
    table = table_ref[...].astype(jnp.float32)
    centred = table - jnp.mean(table, axis=1, keepdims=True)
    variance = jnp.mean(centred * centred, axis=1, keepdims=True)
    normed = (centred * lax.rsqrt(variance + epsilon)).astype(jnp.bfloat16)
    loads[1].wait()
    loads[2].wait()
    rel_query = dot_f32(normed, w_query_ref[...]).astype(jnp.bfloat16)
    rel_query = dot_f32(flip, rel_query).astype(jnp.bfloat16)
    queries = dot_f32(tokens_ref[...], w_query_ref[...])
    query_rows = [
        queries[row : row + 1, chunk * LANES : (chunk + 1) * LANES]
        for row in range(rows_dev)
        for chunk in range(chunks)
    ]
    query_rows.append(jnp.zeros((QROWS - len(query_rows), LANES), jnp.float32))
    query_block = jnp.concatenate(query_rows, axis=0).astype(jnp.bfloat16)
    for chunk in range(chunks):
        at = (chunks + chunk) * pitch
        out_ref[at : at + rows, :] = rel_query[:, chunk * LANES : (chunk + 1) * LANES]
    out_ref[query_at:, :] = query_block
    loads[3].wait()
    rel_key = dot_f32(normed, w_key_ref[...]).astype(jnp.bfloat16)
    for chunk in range(chunks):
        at = chunk * pitch
        out_ref[at : at + rows, :] = rel_key[:, chunk * LANES : (chunk + 1) * LANES]


def longest_first(cache_len_ref):
    rows_dev = cache_len_ref.shape[1]
    lane = lax.broadcasted_iota(jnp.int32, (1, rows_dev), 1)
    cache_len = cache_len_ref[...].astype(jnp.float32)
    lengths = [jnp.sum(jnp.where(lane == slot, cache_len, 0.0)) for slot in range(rows_dev)]
    longest, first = lengths[0], jnp.int32(0)
    for slot in range(1, rows_dev):
        first = jnp.where(lengths[slot] > longest, slot, first)
        longest = jnp.maximum(lengths[slot], longest)
    order, ordered = [first], [longest]
    for place in range(1, rows_dev):
        order.append(jnp.where(first < place, place, place - 1))
        ordered.append(jnp.where(first < place, lengths[place], lengths[place - 1]))
    return order, ordered


def shard_at(by_halves, sources, source):
    if not by_halves:
        return source
    own_half = lax.axis_index("req") // (sources // 2)
    return (own_half ^ (source % 2)) * (sources // 2) + source // 2


def keep_kernel(
    by_halves, chunks, slot_of_ref, cache_len_ref, key_hbm, out_ref, hit_ref, sem
):
    order, _ = longest_first(cache_len_ref)
    load = pltpu.make_async_copy(key_hbm.at[order[0]], out_ref, sem)
    load.start()
    rows_dev, requests = cache_len_ref.shape[1], slot_of_ref.shape[1]
    sources = hit_ref.shape[1] // QROWS
    shard_of = functools.partial(shard_at, by_halves, sources)
    first_slot = lax.axis_index("req") * rows_dev
    places = sources * QROWS
    held = rows_dev * chunks
    request_id = lax.broadcasted_iota(jnp.int32, (requests, places), 0)
    place = lax.broadcasted_iota(jnp.int32, (requests, places), 1)
    place_request = shard_of(place // QROWS) * rows_dev + (place % QROWS) // chunks
    used = (place % QROWS < held) & (place_request == request_id)
    slots = jnp.broadcast_to(slot_of_ref[...].astype(jnp.float32), (QROWS, requests))
    slot_at = dot_f32(slots.astype(jnp.bfloat16), jnp.where(used, 1.0, 0.0).astype(jnp.bfloat16))
    wanted = lax.broadcasted_iota(jnp.int32, (QROWS, places), 0)
    place = lax.broadcasted_iota(jnp.int32, (QROWS, places), 1) % QROWS
    wanted_slot = first_slot + sum(
        jnp.where(wanted // chunks == place_held, order[place_held], 0)
        for place_held in range(rows_dev)
    )
    hit = (
        (slot_at == wanted_slot.astype(jnp.float32))
        & (place % chunks == wanted % chunks)
        & (place < held)
        & (wanted < held)
    )
    hit_ref[...] = jnp.where(hit, 1.0, 0.0).astype(jnp.bfloat16)
    load.wait()


def spread_kernel(own_ref, mirror_ref, out_ref):
    rows = own_ref.shape[0]
    own, mirror = own_ref[...], mirror_ref[...]
    for peer in range(out_ref.shape[0]):
        out_ref[peer, 0:rows, :] = own
        out_ref[peer, rows : 2 * rows, :] = mirror


def split3(value):
    high = value.astype(jnp.bfloat16)
    rest = value - high.astype(jnp.float32)
    middle = rest.astype(jnp.bfloat16)
    low = (rest - middle.astype(jnp.float32)).astype(jnp.bfloat16)
    return high, middle, low


def attend_kernel(
    by_halves, hit_ref, cache_len_ref, table_ref, queries_ref, bucket_ref, first_key_ref, key_hbm, value_hbm,
    out_ref, key_ref, value_ref, rel_key_ref, rel_query_ref, score_ref, key_sems, value_sems,
):
    rows_dev, cols = key_ref.shape[0], key_ref.shape[2]
    heads = cols // HD
    pairs = rows_dev * heads
    chunks = cols // LANES
    shards, shard_rows = table_ref.shape[0], BUCKETS // table_ref.shape[0]
    query_at = queries_ref.shape[1] - QROWS
    first_slot = lax.axis_index("req") * rows_dev

    order, lengths = longest_first(cache_len_ref)

    def load(source, target, sems, place, part):
        rows = pl.ds(part * REGION, REGION)
        return pltpu.make_async_copy(
            source.at[order[place], rows], target.at[place, rows], sems.at[place, part]
        )

    load_keys = functools.partial(load, key_hbm, key_ref, key_sems)
    load_values = functools.partial(load, value_hbm, value_ref, value_sems)
    parts = MAXLEN // REGION

    def start_loads(place, part):
        if place:
            load_keys(place, part).start()
        load_values(place, part).start()

    for place in reversed(range(rows_dev)):
        start_loads(place, 0)

    @pl.when(lengths[0] > REGION)
    def _():
        for part in range(1, parts):
            start_loads(0, part)

    for place in range(1, rows_dev):
        for part in range(1, parts):

            @pl.when(lengths[place] > part * REGION)
            def _():
                start_loads(place, part)

    sources = queries_ref.shape[0]
    shard_of = functools.partial(shard_at, by_halves, sources)

    for source in range(shards):
        shard = shard_of(source)
        rows = pl.ds(shard * shard_rows, shard_rows)
        reversed_rows = pl.ds((shards - 1 - shard) * shard_rows, shard_rows)
        if by_halves:
            rows = pl.ds(pl.multiple_of(rows.start, shard_rows), shard_rows)
            reversed_rows = pl.ds(pl.multiple_of(reversed_rows.start, shard_rows), shard_rows)
        for chunk in range(chunks):
            lanes = slice(chunk * LANES, (chunk + 1) * LANES)
            at = chunk * shard_rows
            rel_key_ref[rows, lanes] = table_ref[source, at : at + shard_rows, :]
            at = (chunks + chunk) * shard_rows
            rel_query_ref[reversed_rows, lanes] = table_ref[source, at : at + shard_rows, :]

    query_rows = jnp.concatenate(
        [queries_ref[source, query_at:, :].astype(jnp.float32) for source in range(sources)], axis=0
    )
    own_queries = dot_f32(
        hit_ref[...], query_rows.astype(jnp.bfloat16)
    )

    pair_id = lax.broadcasted_iota(jnp.int32, (pairs, cols), 0)
    head_id = lax.broadcasted_iota(jnp.int32, (pairs, cols), 1) // HD
    query_heads = jnp.zeros((pairs, cols), jnp.float32)
    query_columns = []
    for index in range(rows_dev):
        own = own_queries[index * chunks : (index + 1) * chunks]
        query = jnp.concatenate([own[chunk : chunk + 1] for chunk in range(chunks)], axis=1)
        query_heads = jnp.where(pair_id == index * heads + head_id, query, query_heads)
        query_columns.append(
            jnp.concatenate(
                [
                    jnp.broadcast_to(own[chunk : chunk + 1], (LANES, LANES)).T
                    for chunk in range(chunks)
                ],
                axis=0,
            )
        )
    by_bucket = lax.dot_general(
        query_heads.astype(jnp.bfloat16), rel_key_ref[...], NT, preferred_element_type=jnp.float32
    )
    shifted = jnp.concatenate((by_bucket[:, 1:], by_bucket[:, :1]), axis=1)
    rel_query = rel_query_ref[...].astype(jnp.float32).T.astype(jnp.bfloat16)
    left = jnp.concatenate((rel_query,) + split3(shifted), axis=0)

    pair_row = lax.broadcasted_iota(jnp.int32, (pairs, 1), 0)
    pair_length = jnp.full((pairs, 1), lengths[0], jnp.float32)
    for index in range(1, rows_dev):
        pair_length = jnp.where(pair_row >= index * heads, lengths[index], pair_length)
    table_id = lax.broadcasted_iota(jnp.int32, (BUCKETS, BLOCK), 0)
    table_half = (table_id - BUCKETS // 2).astype(jnp.bfloat16)

    def block_scores(index, offset):
        here = slice(offset, offset + BLOCK)
        bucket = bucket_ref[pl.ds(order[index], 1), here]
        row = (jnp.maximum(bucket - 1, 0) - BUCKETS // 2).astype(jnp.bfloat16)
        one_hot = jnp.where(table_half == row, jnp.bfloat16(1.0), jnp.bfloat16(0.0))
        found = dot_f32(left, one_hot)
        keys = key_ref[index, here, :] if index else first_key_ref[here, :]
        query_column = jnp.concatenate([query_columns[index]] * (BLOCK // LANES), axis=1)
        products = keys.astype(jnp.float32).T * (found[:cols] + query_column)
        along = found[cols : cols + pairs] + (
            found[cols + pairs : cols + 2 * pairs] + found[cols + 2 * pairs :]
        )
        along = jnp.where(bucket == 0, by_bucket[:, 0:1], along)
        sums = [
            jnp.sum(products[head * HD : (head + 1) * HD], axis=0, keepdims=True)
            for head in range(heads)
        ]
        own_pairs = slice(index * heads, (index + 1) * heads)
        score_ref[own_pairs, here] = jnp.concatenate(sums, axis=0) + along[own_pairs]

    def attend(sizes):
        width = max(sizes)
        for index in range(rows_dev):
            own_pairs = slice(index * heads, (index + 1) * heads)
            if sizes[index] < width:
                score_ref[own_pairs, sizes[index] : width] = jnp.zeros(
                    (heads, width - sizes[index]), jnp.float32
                )
            for offset in range(0, sizes[index], BLOCK):
                if index and offset % REGION == 0:
                    load_keys(index, offset // REGION).wait()
                block_scores(index, offset)
        place = lax.broadcasted_iota(jnp.int32, (pairs, width), 1)
        live = place.astype(jnp.float32) < pair_length
        scores = score_ref[:, 0:width] * (1.0 / math.sqrt(3.0 * HD))
        scores = jnp.where(live, scores, masked_score)
        highest = jnp.max(scores, axis=1, keepdims=True)
        exponent = jnp.where(live, jnp.exp(scores - highest), 0.0)
        weights = (exponent / jnp.sum(exponent, axis=1, keepdims=True)).astype(jnp.bfloat16)
        contexts = [jnp.zeros((1, cols), jnp.float32)] * rows_dev
        for index in range(rows_dev):
            size = sizes[index]
            for part in range(size // REGION):
                load_values(index, part).wait()
            spread = dot_f32(weights[:, 0:size], value_ref[index, 0:size, :])
            spread = jnp.where(pair_id == index * heads + head_id, spread, 0.0)
            context = jnp.sum(spread, axis=0, keepdims=True)
            contexts = [
                jnp.where(order[index] == row, context, other)
                for row, other in enumerate(contexts)
            ]
        context = jnp.concatenate(contexts, axis=0).astype(jnp.bfloat16)
        out_ref[...] = jnp.broadcast_to(context[None], out_ref.shape)

    steps = range(REGION, MAXLEN + 1, REGION)
    for sizes in itertools.product((REGION, MAXLEN), *[steps] * (rows_dev - 1)):
        if max(sizes) > sizes[0]:
            continue
        taken = (lengths[0] > REGION) == (sizes[0] > REGION)
        for index in range(1, rows_dev):
            taken &= lengths[index] > sizes[index] - REGION
            taken &= lengths[index] <= sizes[index]
        pl.when(taken)(functools.partial(attend, sizes))


def finish_kernel(tp_size, slot_of_ref, contexts_ref, tokens_ref, gain_ref, bias_ref, *refs):
    w_refs, (out_ref, norm_ref) = refs[:tp_size], refs[tp_size:]
    rows_dev, width = tokens_ref.shape
    cols = out_ref.shape[1]
    requests = slot_of_ref.shape[1]
    first_row = lax.axis_index("req") * rows_dev
    tp_index = lax.axis_index("tp")
    lane = lax.broadcasted_iota(jnp.int32, (8, requests), 1)
    row = lax.broadcasted_iota(jnp.int32, (8, requests), 0)
    slots = jnp.broadcast_to(slot_of_ref[...].astype(jnp.float32), (8, requests))
    slot = jnp.sum(jnp.where(lane == first_row + row, slots, 0.0), axis=1, keepdims=True)
    chosen = jnp.where(lane.astype(jnp.float32) == slot, 1.0, 0.0).astype(jnp.bfloat16)
    products = []
    gathered = jnp.concatenate(
        [
            jnp.concatenate(
                [
                    contexts_ref[source * tp_size + (tp_index ^ step)].astype(jnp.float32)
                    for source in range(requests // rows_dev)
                ],
                axis=0,
            )
            for step in range(tp_size)
        ],
        axis=1,
    )
    context = dot_f32(chosen, gathered.astype(jnp.bfloat16)).astype(jnp.bfloat16)
    for step in range(tp_size):
        products.append(dot_f32(context[:, step * cols : (step + 1) * cols], w_refs[step][...]))
    while len(products) > 1:
        products = [a + b for a, b in zip(products[::2], products[1::2], strict=True)]
    product = products[0]
    attended = product[0:rows_dev] + tokens_ref[...].astype(jnp.float32)
    mean = jnp.mean(attended, axis=1, keepdims=True)
    centred = attended - mean
    variance = jnp.mean(centred * centred, axis=1, keepdims=True)
    norm_ref[...] = centred * lax.rsqrt(variance + epsilon)
    own_cols = norm_ref[:, pl.ds(pl.multiple_of(tp_index * cols, cols), cols)]
    out_ref[...] = (own_cols * gain_ref[...] + bias_ref[...]).astype(out_ref.dtype)


def xor_permute(block, tp_size, bit):
    return lax.ppermute(block, "tp", [(i, i ^ bit) for i in range(tp_size)])


def gather_half(block, tp_size):
    return {0: block, 2: xor_permute(block, tp_size, 2), 1: xor_permute(block, tp_size, 1)}


def complete(held, tp_size):
    return [held[0], held[1], held[2], xor_permute(held[2], tp_size, 1)]


def make_per_device(req_size, tp_size):
    def per_device(
        tokens,
        slot_of,
        key_cache,
        value_cache,
        cache_len,
        rel_bucket,
        rel_table,
        w_query,
        w_key,
        w_out,
        out_gain,
        out_bias,
    ):
        rows_dev, width = tokens.shape
        slots = slot_of.reshape(1, -1)
        cols = w_query.shape[1]
        chunks = cols // LANES
        shard_rows = rel_table.shape[0]
        pitch = -(-shard_rows // 8) * 8
        table_rows = 2 * chunks * pitch
        block_rows = table_rows + QROWS
        block = pl.pallas_call(
            project_kernel,
            out_shape=jax.ShapeDtypeStruct((block_rows, LANES), jnp.bfloat16),
            in_specs=[ANY] * 4,
            out_specs=VMEM,
            scratch_shapes=[
                pltpu.VMEM(tokens.shape, jnp.bfloat16),
                pltpu.VMEM(rel_table.shape, jnp.bfloat16),
                pltpu.VMEM(w_query.shape, jnp.bfloat16),
                pltpu.VMEM(w_key.shape, jnp.bfloat16),
                pltpu.SemaphoreType.DMA((4,)),
            ],
            name="project",
            compiler_params=ROOM,
        )(*[in_hbm(array) for array in (tokens, rel_table, w_query, w_key)])
        half = req_size // 2
        mirror = lax.ppermute(block, "req", [(i, (i + half) % req_size) for i in range(req_size)])
        send = pl.pallas_call(
            spread_kernel,
            out_shape=jax.ShapeDtypeStruct((half, 2 * block_rows, LANES), jnp.bfloat16),
            in_specs=[VMEM] * 2,
            out_specs=VMEM,
            name="spread",
            compiler_params=ROOM,
        )(block, mirror)
        halves = [list(range(half)), list(range(half, req_size))]
        received = lax.all_to_all(send, "req", 0, 0, axis_index_groups=halves)
        w_blocks = gather_half(lax.optimization_barrier((block, w_out))[1], tp_size)
        received = received.reshape(req_size, block_rows, LANES)
        by_halves = shard_rows % 16 == 0
        if by_halves:
            table = received
        else:
            received = received.reshape(half, 2, block_rows, LANES).transpose(1, 0, 2, 3)
            first = lax.axis_index("req") < half
            received = jnp.where(first, received, received[::-1])
            received = received.reshape(req_size, block_rows, LANES)
            table = received[:, :table_rows].reshape(req_size, 2, chunks, pitch, LANES)
            table = table[:, :, :, :shard_rows]
            table = jnp.stack((table[:, 0], table[::-1, 1]), axis=0)
            table = table.transpose(0, 2, 1, 3, 4).reshape(1, -1, LANES)
        lengths = cache_len.reshape(1, rows_dev)
        first_key, hit = pl.pallas_call(
            functools.partial(keep_kernel, by_halves, chunks),
            out_shape=[
                pltpu.VMEM(key_cache.shape[1:], key_cache.dtype),
                pltpu.VMEM((QROWS, req_size * QROWS), jnp.bfloat16),
            ],
            in_specs=[VMEM, VMEM, ANY],
            out_specs=[VMEM] * 2,
            scratch_shapes=[pltpu.SemaphoreType.DMA],
            name="keep",
            compiler_params=ROOM,
        )(slots, lengths, in_hbm(key_cache))
        contexts = pl.pallas_call(
            functools.partial(attend_kernel, by_halves),
            out_shape=jax.ShapeDtypeStruct((req_size * tp_size, rows_dev, cols), jnp.bfloat16),
            in_specs=[VMEM] * 6 + [ANY, ANY],
            out_specs=VMEM,
            scratch_shapes=[
                pltpu.VMEM(key_cache.shape, jnp.bfloat16),
                pltpu.VMEM(value_cache.shape, jnp.bfloat16),
                pltpu.VMEM((BUCKETS, cols), jnp.bfloat16),
                pltpu.VMEM((BUCKETS, cols), jnp.bfloat16),
                pltpu.VMEM((rows_dev * cols // HD, MAXLEN), jnp.float32),
                pltpu.SemaphoreType.DMA((rows_dev, MAXLEN // REGION)),
                pltpu.SemaphoreType.DMA((rows_dev, MAXLEN // REGION)),
            ],
            name="attend",
            compiler_params=ROOM,
        )(
            hit,
            lengths,
            table,
            received,
            rel_bucket,
            first_key,
            in_hbm(key_cache),
            in_hbm(value_cache),
        )
        contexts, w_blocks = lax.optimization_barrier((contexts, complete(w_blocks, tp_size)))
        contexts = lax.all_to_all(contexts, ("req", "tp"), 0, 0)
        return pl.pallas_call(
            functools.partial(finish_kernel, tp_size),
            out_shape=jax.ShapeDtypeStruct((rows_dev, cols), jnp.bfloat16),
            in_specs=[VMEM] * (5 + tp_size),
            out_specs=VMEM,
            scratch_shapes=[pltpu.VMEM((rows_dev, width), jnp.float32)],
            name="finish",
            compiler_params=ROOM,
        )(
            slots,
            contexts,
            tokens,
            out_gain.reshape(1, cols),
            out_bias.reshape(1, cols),
            *[in_vmem(block) for block in w_blocks],
        )

    return per_device


def solution(mesh):
    in_specs = (
        P("req", None),
        P(),
        P("req", None, "tp"),
        P("req", None, "tp"),
        P("req"),
        P("req", None),
        P("req", None),
        P(None, "tp"),
        P(None, "tp"),
        P("tp", None),
        P("tp"),
        P("tp"),
    )
    return jax.shard_map(
        make_per_device(mesh.shape["req"], mesh.shape["tp"]),
        mesh=mesh,
        in_specs=in_specs,
        out_specs=P("req", "tp"),
        check_vma=False,
    )
```
